32 devices in a mesh: fsdp: 8 (over y, x, core), tp: 4 (over z).
Axes of the slice: x: 2, y: 2, z: 4, core: 2. Of those that a mesh axis runs over, the one named last changes fastest.
Arguments:
- hidden_in: bfloat16 [2, 8192, 2048], P(None, ('fsdp', 'tp')), may hold values from -27 to 27
- out_grad: bfloat16 [2, 8192, 2048], P(None, ('fsdp', 'tp')), may hold values from -6 to 6
- lengths: int32 [2, 8], P(None, 'fsdp'), may hold values from 256 to 1024, as said below
- qkv_weight: bfloat16 [2048, 6144], P('fsdp', 'tp'), may hold values from -0.125 to 0.125
- qkv_bias: bfloat16 [6144], P(('tp', 'fsdp')), may hold values from -3 to 3
- out_weight: bfloat16 [2048, 2048], P('tp', 'fsdp'), may hold values from -0.5 to 0.5
- out_bias: bfloat16 [2048], P('fsdp'), may hold values from -3 to 3
- fc1_weight: bfloat16 [2048, 8192], P('fsdp', 'tp'), may hold values from -0.125 to 0.125
- fc1_bias: bfloat16 [8192], P(('tp', 'fsdp')), may hold values from -3 to 3
- fc2_weight: bfloat16 [8192, 2048], P('tp', 'fsdp'), may hold values from -0.0625 to 0.0625
- fc2_bias: bfloat16 [2048], P('fsdp'), may hold values from -3 to 3
- ln1_gain: bfloat16 [2048], P('fsdp'), may hold values from 0.5 to 1.5
- ln1_bias: bfloat16 [2048], P('fsdp'), may hold values from -2 to 2
- ln2_gain: bfloat16 [2048], P('fsdp'), may hold values from 0.5 to 1.5
- ln2_bias: bfloat16 [2048], P('fsdp'), may hold values from -2 to 2
Outputs:
- hidden_out: bfloat16 [2, 8192, 2048], P(None, ('fsdp', 'tp'))
- in_grad: bfloat16 [2, 8192, 2048], P(None, ('fsdp', 'tp'))
- grad_qkv_weight: float32 [2048, 6144], P('fsdp', 'tp')
- grad_qkv_bias: float32 [6144], P(('tp', 'fsdp'))
- grad_out_weight: float32 [2048, 2048], P('tp', 'fsdp')
- grad_out_bias: float32 [2048], P('fsdp')
- grad_fc1_weight: float32 [2048, 8192], P('fsdp', 'tp')
- grad_fc1_bias: float32 [8192], P(('tp', 'fsdp'))
- grad_fc2_weight: float32 [8192, 2048], P('tp', 'fsdp')
- grad_fc2_bias: float32 [2048], P('fsdp')
- grad_ln1_gain: float32 [2048], P('fsdp')
- grad_ln1_bias: float32 [2048], P('fsdp')
- grad_ln2_gain: float32 [2048], P('fsdp')
- grad_ln2_bias: float32 [2048], P('fsdp')
The draws below stay inside these ranges and needn't reach their ends.
Inputs may be any that keep to these rules, and one draw needn't show every extreme that they name: `lengths`: in every micro-batch some slot holds a sequence of 1024 rows.
All inputs are finite; a program needn't handle non-finite values.
Results may differ from the reference program's by a relative error of at most 0.0097.
Values may be sent and summed in bfloat16 or wider, within the bound.
A program may use at most 320 MiB of HBM per device.

```python
import math
import jax
import jax.numpy as jnp
from jax import lax

D = 2048
H = 16
HEAD = 128
FF = 8192
ROT = 32
SLOT = 1024
MB = 2
TOKENS = 8192


def draw_hidden_in(key, part):
    row_scale = jnp.exp(jax.random.uniform(jax.random.fold_in(key, 11), (MB, TOKENS, 1), minval=-1.15, maxval=1.15))
    column_scale = jnp.exp(jax.random.uniform(jax.random.fold_in(key, 12), (1, 1, D), minval=-0.5, maxval=0.5))
    base = jax.random.normal(jax.random.fold_in(key, 13), (MB, TOKENS, D))
    base = jnp.clip(base, -5.0, 5.0)
    return (base * row_scale * column_scale).astype(jnp.bfloat16)


def draw_lengths(key, part):
    slot_count = TOKENS // SLOT
    drawn = jax.random.randint(jax.random.fold_in(key, 21), (MB, slot_count), SLOT // 4, SLOT + 1)
    chosen = jax.random.randint(jax.random.fold_in(key, 22), (MB, 1), 0, slot_count)
    filled = jnp.arange(slot_count)[None, :] == chosen
    return jnp.where(filled, SLOT, drawn).astype(jnp.int32)


def level_of(key, dims, cuts, least, high):
    factor_of, own = 1.0, jax.random.fold_in(key, 6)
    for axis_at, blocks in cuts:
        draws = jnp.exp(jax.random.uniform(jax.random.fold_in(own, axis_at), (blocks,), jnp.float32, least / len(cuts), high / len(cuts)))
        factor_of = factor_of * jnp.repeat(draws, dims[axis_at] // blocks).reshape([-1 if axis == axis_at else 1 for axis in range(len(dims))])
    return factor_of


def normal_values(rng, extent, scale, most, pieces=(), held_as=jnp.bfloat16):
    values = scale * jax.random.normal(rng, extent, jnp.float32)
    if pieces:
        values = values * level_of(rng, extent, pieces, -0.22, 0.18)
    return jnp.clip(values, -most, most).astype(held_as)


def setup_inputs(seed: int = 0) -> dict:
    seeds = jax.random.split(jax.random.key(seed), 16)
    hidden_in = draw_hidden_in(jax.random.fold_in(seeds[15], 71), 0)
    out_grad = normal_values(seeds[1], (MB, TOKENS, D), 1.0, 6.0, ((1, 32),))
    lengths = draw_lengths(jax.random.fold_in(seeds[15], 71), 0)
    qkv_weight = normal_values(seeds[3], (D, 3 * D), D ** -0.5, 0.125, ((0, 8), (1, 4)))
    qkv_bias = normal_values(seeds[4], (3 * D,), 0.5, 3.0, ((0, 32),))
    out_weight = normal_values(seeds[5], (D, D), (D // 16) ** -0.5, 0.5, ((0, 4), (1, 8)))
    out_bias = normal_values(seeds[6], (D,), 0.5, 3.0, ((0, 8),))
    fc1_weight = normal_values(seeds[7], (D, FF), D ** -0.5, 0.125, ((0, 8), (1, 4)))
    fc1_bias = normal_values(seeds[8], (FF,), 0.5, 3.0, ((0, 32),))
    fc2_weight = normal_values(seeds[9], (FF, D), FF ** -0.5, 0.0625, ((0, 4), (1, 8)))
    fc2_bias = normal_values(seeds[10], (D,), 0.5, 3.0, ((0, 8),))
    ln1_gain = jnp.clip(1.0 + 0.1 * jax.random.normal(seeds[11], (D,), jnp.float32), 0.5, 1.5).astype(jnp.bfloat16)
    ln1_bias = normal_values(seeds[12], (D,), 0.3, 2.0, ((0, 8),))
    ln2_gain = jnp.clip(1.0 + 0.1 * jax.random.normal(seeds[13], (D,), jnp.float32), 0.5, 1.5).astype(jnp.bfloat16)
    ln2_bias = normal_values(seeds[14], (D,), 0.3, 2.0, ((0, 8),))
    return {"hidden_in": hidden_in, "out_grad": out_grad, "lengths": lengths, "qkv_weight": qkv_weight, "qkv_bias": qkv_bias, "out_weight": out_weight, "out_bias": out_bias, "fc1_weight": fc1_weight, "fc1_bias": fc1_bias, "fc2_weight": fc2_weight, "fc2_bias": fc2_bias, "ln1_gain": ln1_gain, "ln1_bias": ln1_bias, "ln2_gain": ln2_gain, "ln2_bias": ln2_bias}


EPSILON = 1e-05
MASKED = -1e+30

@jax.custom_vjp
def low(v):
    return lax.optimization_barrier(v.astype(jnp.bfloat16)).astype(jnp.float32)

@jax.custom_vjp
def low_back(v):
    return v

def low_keep(v):
    return (low(v), None)

def low_pass(kept, grad):
    return (grad,)

def back_keep(v):
    return (v, None)

def back_low(kept, grad):
    return (low(grad),)
low.defvjp(low_keep, low_pass)
low_back.defvjp(back_keep, back_low)

def layer_norm(row_block, norm_gain, norm_shift):
    row_mean = lax.optimization_barrier(jnp.mean(row_block, axis=-1, keepdims=True))
    centred = row_block - row_mean
    spread = lax.optimization_barrier(jnp.mean(centred * centred, axis=-1, keepdims=True))
    return centred * lax.rsqrt(spread + EPSILON) * norm_gain + norm_shift

def rotary_tables(row_count, rot_width):
    exponent = jnp.arange(0, rot_width, 2).astype(jnp.float32) / rot_width
    inverse = 1.0 / 10000.0 ** exponent
    places = jnp.arange(row_count).astype(jnp.float32)
    angles = places[:, None] * inverse[None, :]
    angles = jnp.concatenate([angles, angles], axis=-1)
    return (jnp.cos(angles)[:, None, :], jnp.sin(angles)[:, None, :])

def rotate(head_block, cosine_table, sine_table, rot_width):
    half_width = rot_width // 2
    turning = head_block[..., :rot_width]
    turned = jnp.concatenate([-turning[..., half_width:], turning[..., :half_width]], axis=-1)
    return jnp.concatenate([turning * cosine_table + turned * sine_table, head_block[..., rot_width:]], axis=-1)

def matmul(first_arr, second_arr):
    return jnp.dot(first_arr, second_arr, precision=lax.Precision.HIGHEST, preferred_element_type=jnp.float32)

def slot_forward(slot_input, length, weight_set):
    qkv_weight, qkv_bias, out_weight, out_bias, fc1_weight, fc1_bias, fc2_weight, fc2_bias, ln1_gain, ln1_bias, ln2_gain, ln2_bias = weight_set
    normed_one = low(layer_norm(slot_input, ln1_gain, ln1_bias))
    normed_two = low(layer_norm(slot_input, ln2_gain, ln2_bias))
    projected = low_back(matmul(normed_one, qkv_weight) + qkv_bias)
    projected = projected.reshape(SLOT, H, 3, HEAD)
    cosine_table, sine_table = rotary_tables(SLOT, ROT)
    queries = low(rotate(projected[:, :, 0], cosine_table, sine_table, ROT))
    keys_all = low(rotate(projected[:, :, 1], cosine_table, sine_table, ROT))
    values_all = low(projected[:, :, 2])
    row_ids = jnp.arange(SLOT)
    block_rows = min(512, SLOT)
    block_count = SLOT // block_rows
    score_scale = 1.0 / math.sqrt(HEAD)

    def attend_block(scanned):
        query_block, start_row = scanned
        scores = jnp.einsum('qhd,khd->hqk', query_block, keys_all, precision=lax.Precision.HIGHEST) * score_scale
        query_rows = start_row + jnp.arange(block_rows)
        allowed = (row_ids[None, :] <= query_rows[:, None]) & (row_ids[None, :] < length)
        scores = low_back(jnp.where(allowed[None], scores, MASKED))
        row_top = lax.optimization_barrier(jnp.max(scores, axis=-1, keepdims=True))
        raised = jnp.exp(scores - row_top)
        prob_rows = low(raised / lax.optimization_barrier(jnp.sum(raised, axis=-1, keepdims=True)))
        return jnp.einsum('hqk,khd->qhd', prob_rows, values_all, precision=lax.Precision.HIGHEST)
    query_blocks = queries.reshape(block_count, block_rows, H, HEAD)
    block_starts = (jnp.arange(block_count) * block_rows).astype(jnp.int32)
    mixed_rows = lax.map(jax.checkpoint(attend_block), (query_blocks, block_starts))
    attended = low(low_back(mixed_rows.reshape(SLOT, D)))
    pre_act = low_back(matmul(normed_two, fc1_weight) + fc1_bias)
    activated = low(jax.nn.gelu(pre_act, approximate=False))
    valid = (row_ids < length).astype(jnp.float32)[:, None]
    return valid * (slot_input + matmul(attended, out_weight) + out_bias + matmul(activated, fc2_weight) + fc2_bias)

def reference(hidden_in, out_grad, lengths, qkv_weight, qkv_bias, out_weight, out_bias, fc1_weight, fc1_bias, fc2_weight, fc2_bias, ln1_gain, ln1_bias, ln2_gain, ln2_bias):
    weight_set = tuple((weight_arr.astype(jnp.float32) for weight_arr in (qkv_weight, qkv_bias, out_weight, out_bias, fc1_weight, fc1_bias, fc2_weight, fc2_bias, ln1_gain, ln1_bias, ln2_gain, ln2_bias)))
    slot_total = MB * (TOKENS // SLOT)
    slot_inputs = hidden_in.astype(jnp.float32).reshape(slot_total, SLOT, D)
    slot_cots = out_grad.astype(jnp.float32).reshape(slot_total, SLOT, D)
    slot_lengths = lengths.reshape(slot_total).astype(jnp.int32)

    def one_slot(totals, scanned):
        slot_input, slot_cot, length = scanned

        def forward(inputs_f, weights_f):
            return slot_forward(inputs_f, length, weights_f)
        result, pullback = jax.vjp(forward, slot_input, weight_set)
        grad_rows, grad_weights = pullback(slot_cot)
        totals = jax.tree.map(jnp.add, totals, grad_weights)
        return (totals, (result.astype(jnp.bfloat16), grad_rows.astype(jnp.bfloat16)))
    zero_grads = jax.tree.map(jnp.zeros_like, weight_set)
    totals, (results, grads_in) = lax.scan(one_slot, zero_grads, (slot_inputs, slot_cots, slot_lengths))
    return (results.reshape(MB, TOKENS, D), grads_in.reshape(MB, TOKENS, D), totals[0], totals[1], totals[2], totals[3], totals[4], totals[5], totals[6], totals[7], totals[8], totals[9], totals[10], totals[11])
```

```python
from functools import partial
import math

import jax
import jax.numpy as jnp
from jax import lax
from jax.experimental import pallas as pl
from jax.experimental.pallas import tpu as pltpu
from jax.sharding import PartitionSpec as P

HEAD = 128
ROT = 32
EPSILON = 1e-05
MASKED = -1e30
F32 = jnp.float32
BF16 = jnp.bfloat16
VMEM_BYTES = 60 << 20


def dot_nn(a, b):
    return lax.dot_general(a, b, (((1,), (0,)), ((), ())), preferred_element_type=F32)


def dot_nt(a, b):
    return lax.dot_general(a, b, (((1,), (1,)), ((), ())), preferred_element_type=F32)


def dot_tn(a, b):
    return lax.dot_general(a, b, (((0,), (0,)), ((), ())), preferred_element_type=F32)


def row_stats(rows):
    mean = jnp.mean(rows, axis=-1, keepdims=True)
    centred = rows - mean
    spread = jnp.mean(centred * centred, axis=-1, keepdims=True)
    rstd = lax.rsqrt(spread + EPSILON)
    return centred * rstd, rstd


def rotary_full(row_count):
    half = ROT // 2
    exponent = jnp.arange(0, ROT, 2).astype(F32) / ROT
    inverse = 1.0 / 10000.0**exponent
    angles = jnp.arange(row_count).astype(F32)[:, None] * inverse[None, :]
    cosine, sine = jnp.cos(angles), jnp.sin(angles)
    rest = jnp.ones((row_count, HEAD - ROT), F32)
    return (
        jnp.concatenate([cosine, cosine, rest], axis=1),
        jnp.concatenate([-sine, sine, 0.0 * rest], axis=1),
    )


def swap_halves(block):
    half = ROT // 2
    lane = lax.broadcasted_iota(jnp.int32, block.shape, 1)
    return jnp.where(lane < half, pltpu.roll(block, HEAD - half, 1), pltpu.roll(block, half, 1))


def attention_kernel(
    row_tiles, heads, tile, len_ref, x_ref, c_ref, wqkv_ref, bqkv_ref, wo_ref, gain_ref, shift_ref,
    cos_ref, sin_ref, n1_ref, att_ref, gp_ref, q_s, k_s, v_s, ga_s, dk_s, dv_s,
):
    step = pl.program_id(0)
    length = len_ref[0]
    scale = 1.0 / math.sqrt(HEAD)

    @pl.when(step < row_tiles)
    def _():
        rows = pl.ds(pl.multiple_of(step * tile, tile), tile)
        xhat, _ = row_stats(x_ref[...].astype(F32))
        normed = (xhat * gain_ref[...] + shift_ref[...]).astype(BF16)
        n1_ref[...] = normed
        cosine, sine = cos_ref[rows, :], sin_ref[rows, :]
        for h in range(heads):
            part = dot_nn(normed, wqkv_ref[:, h * 384:(h + 1) * 384]) + bqkv_ref[:, h * 384:(h + 1) * 384]
            q, k = part[:, :HEAD], part[:, HEAD:2 * HEAD]
            q_s[h, rows, :] = (q * cosine + swap_halves(q) * sine).astype(BF16)
            k_s[h, rows, :] = (k * cosine + swap_halves(k) * sine).astype(BF16)
            v_s[h, rows, :] = part[:, 2 * HEAD:].astype(BF16)
        place = step * tile + lax.broadcasted_iota(jnp.int32, c_ref.shape, 0)
        cot = jnp.where(place < length, c_ref[...], jnp.zeros_like(c_ref))
        width = wo_ref.shape[2]
        grad = jnp.zeros((tile, heads * HEAD), F32)
        for j in range(wo_ref.shape[0]):
            grad = grad + dot_nt(cot[:, j * width:(j + 1) * width], wo_ref[j])
        for h in range(heads):
            ga_s[h, rows, :] = grad[:, h * HEAD:(h + 1) * HEAD].astype(BF16)

    @pl.when(step >= row_tiles)
    def _():
        h = step - row_tiles
        dk_s[...] = jnp.zeros_like(dk_s)
        dv_s[...] = jnp.zeros_like(dv_s)
        for i in range(row_tiles):
            rows = slice(i * tile, (i + 1) * tile)
            seen = slice(0, (i + 1) * tile)
            q, k, v, ga = q_s[h, rows, :], k_s[h, seen, :], v_s[h, seen, :], ga_s[h, rows, :]
            scores = dot_nt(q, k) * scale
            place = i * tile + lax.broadcasted_iota(jnp.int32, scores.shape, 0)
            key = lax.broadcasted_iota(jnp.int32, scores.shape, 1)
            scores = jnp.where(key <= jnp.minimum(place, length - 1), scores, MASKED)
            top = jnp.max(scores, axis=-1, keepdims=True)
            raised = jnp.exp(scores - top)
            soft = raised * (1.0 / jnp.sum(raised, axis=-1, keepdims=True))
            probs = soft.astype(BF16)
            att_ref[rows, :] = dot_nn(probs, v).astype(BF16)
            grad_probs = dot_nt(ga, v)
            row_dot = jnp.sum(soft * grad_probs, axis=-1, keepdims=True)
            grad_scores = (soft * (grad_probs - row_dot)).astype(BF16)
            dq = dot_nn(grad_scores, k) * scale
            cosine, sine = cos_ref[rows, :], sin_ref[rows, :]
            gp_ref[rows, 0:HEAD] = (dq * cosine - swap_halves(dq) * sine).astype(BF16)
            dk_s[seen, :] += dot_tn(grad_scores, q)
            dv_s[seen, :] += dot_tn(probs, ga)
        dk = dk_s[...] * scale
        gp_ref[:, HEAD:2 * HEAD] = (dk * cos_ref[...] - swap_halves(dk) * sin_ref[...]).astype(BF16)
        gp_ref[:, 2 * HEAD:] = dv_s[...].astype(BF16)


def whole(shape):
    return pl.BlockSpec(shape, lambda i: (0,) * len(shape), pipeline_mode=pl.Buffered(1))


def attention_call(length, x, c, wqkv, bqkv, wo, gain, shift, cos, sin):
    slot, width = x.shape
    heads = wqkv.shape[1] // (3 * HEAD)
    tile = 256
    row_tiles = slot // tile
    row_block = pl.BlockSpec((tile, width), lambda i: (jnp.minimum(i, row_tiles - 1), 0))
    head_at = lambda i: (0, jnp.maximum(i - row_tiles, 0))
    return pl.pallas_call(
        partial(attention_kernel, row_tiles, heads, tile),
        grid=(row_tiles + heads,),
        in_specs=[
            pl.BlockSpec(memory_space=pltpu.SMEM), row_block, row_block, whole(wqkv.shape), whole(bqkv.shape),
            whole(wo.shape), whole(gain.shape), whole(shift.shape), whole(cos.shape), whole(sin.shape),
        ],
        out_specs=[row_block, pl.BlockSpec((slot, HEAD), head_at), pl.BlockSpec((slot, 3 * HEAD), head_at)],
        out_shape=[
            jax.ShapeDtypeStruct((slot, width), BF16),
            jax.ShapeDtypeStruct((slot, heads * HEAD), BF16),
            jax.ShapeDtypeStruct((slot, heads * 3 * HEAD), BF16),
        ],
        scratch_shapes=[pltpu.VMEM((heads, slot, HEAD), BF16)] * 4 + [pltpu.VMEM((slot, HEAD), F32)] * 2,
        compiler_params=pltpu.CompilerParams(
            dimension_semantics=("arbitrary",), vmem_limit_bytes=VMEM_BYTES
        ),
        cost_estimate=pl.CostEstimate(flops=int(14e9), bytes_accessed=int(20e6), transcendentals=int(3e6)),
    )(length, x, c, wqkv, bqkv, wo, gain, shift, cos, sin)


def normal_pair(value):
    density = jnp.exp(-0.5 * value * value)
    t = 1.0 / (1.0 + (0.3275911 * math.sqrt(0.5)) * jnp.abs(value))
    series = ((((1.061405429 * t - 1.453152027) * t) + 1.421413741) * t - 0.284496736) * t + 0.254829592
    tail = (0.5 * t) * series * density
    return jnp.where(value >= 0, 1.0 - tail, tail), density * (1.0 / math.sqrt(2.0 * math.pi))


def feed_kernel(
    tile, chunk, len_ref, x_ref, c_ref, att_ref, gp_ref, w1_ref, w2_ref, wo_ref, wqkv_ref, b1_ref,
    gain1_ref, gain2_ref, shift2_ref, n2_ref, act_ref, gpre_ref, h_ref, u_ref, sd_ref, sf_ref, sq_ref, xhat_s, cot_s,
):
    step = pl.program_id(0)
    length = len_ref[0]
    blocks, hidden, width = w2_ref.shape
    model = x_ref.shape[1]

    @pl.when(step == 0)
    def _():
        sd_ref[...] = jnp.zeros_like(sd_ref)
        sf_ref[...] = jnp.zeros_like(sf_ref)
        sq_ref[...] = jnp.zeros_like(sq_ref)

    xhat, _ = row_stats(x_ref[...].astype(F32))
    xhat_s[...] = xhat
    n2_ref[...] = (xhat * gain2_ref[...] + shift2_ref[...]).astype(BF16)
    place = step * tile + lax.broadcasted_iota(jnp.int32, c_ref.shape, 0)
    cot_s[...] = jnp.where(place < length, c_ref[...], jnp.zeros_like(c_ref))
    ones = jnp.ones((8, tile), BF16)
    for k in range(hidden // chunk):
        cols = slice(k * chunk, (k + 1) * chunk)
        pre = dot_nn(n2_ref[...], w1_ref[:, cols]) + b1_ref[:, cols]
        below, density = normal_pair(pre)
        act_ref[:, cols] = (pre * below).astype(BF16)
        gact = dot_nt(cot_s[:, 0:width], w2_ref[0, cols, :])
        for j in range(1, blocks):
            gact = gact + dot_nt(cot_s[:, j * width:(j + 1) * width], w2_ref[j, cols, :])
        gpre = (gact * (below + pre * density)).astype(BF16)
        gpre_ref[:, cols] = gpre
        sf_ref[:, cols] += dot_nn(ones, gpre)
    sq_ref[...] += dot_nn(ones, gp_ref[...])
    for j in range(blocks):
        cols = slice(j * width, (j + 1) * width)
        h_ref[:, cols] = (dot_nn(act_ref[...], w2_ref[j]) + dot_nn(att_ref[...], wo_ref[j])).astype(BF16)
    for k in range(model // chunk):
        cols = slice(k * chunk, (k + 1) * chunk)
        g2 = dot_nt(gpre_ref[...], w1_ref[cols, :])
        g1 = dot_nt(gp_ref[...], wqkv_ref[cols, :])
        u_ref[:, cols] = (g1 * gain1_ref[:, cols] + g2 * gain2_ref[:, cols]).astype(BF16)
        hat = xhat_s[:, cols]
        sd_ref[0:1, cols] += jnp.sum(g1 * hat, axis=0, keepdims=True)
        sd_ref[1:2, cols] += jnp.sum(g1, axis=0, keepdims=True)
        sd_ref[2:3, cols] += jnp.sum(g2 * hat, axis=0, keepdims=True)
        sd_ref[3:4, cols] += jnp.sum(g2, axis=0, keepdims=True)
        sd_ref[4:5, cols] += dot_nn(ones, cot_s[:, cols])[0:1]


def feed_call(length, x, c, att, gp, w1, w2, wo, wqkv, b1, gain1, gain2, shift2):
    slot, width = x.shape
    hidden = w1.shape[1]
    tile, chunk = 256, 512
    at = lambda i: (i, 0)
    keep = lambda i: (0, 0)
    row_block = pl.BlockSpec((tile, width), at)
    hid_block = pl.BlockSpec((tile, hidden), at)
    return pl.pallas_call(
        partial(feed_kernel, tile, chunk),
        grid=(slot // tile,),
        in_specs=[
            pl.BlockSpec(memory_space=pltpu.SMEM), row_block, row_block, pl.BlockSpec((tile, att.shape[1]), at),
            pl.BlockSpec((tile, gp.shape[1]), at), whole(w1.shape), whole(w2.shape), whole(wo.shape),
            whole(wqkv.shape), whole(b1.shape), whole(gain1.shape), whole(gain2.shape), whole(shift2.shape),
        ],
        out_specs=[
            row_block, hid_block, hid_block, row_block, row_block,
            pl.BlockSpec((8, width), keep), pl.BlockSpec((8, hidden), keep), pl.BlockSpec((8, gp.shape[1]), keep),
        ],
        out_shape=[
            jax.ShapeDtypeStruct((slot, width), BF16),
            jax.ShapeDtypeStruct((slot, hidden), BF16),
            jax.ShapeDtypeStruct((slot, hidden), BF16),
            jax.ShapeDtypeStruct((slot, width), BF16),
            jax.ShapeDtypeStruct((slot, width), BF16),
            jax.ShapeDtypeStruct((8, width), F32),
            jax.ShapeDtypeStruct((8, hidden), F32),
            jax.ShapeDtypeStruct((8, gp.shape[1]), F32),
        ],
        scratch_shapes=[pltpu.VMEM((tile, width), F32), pltpu.VMEM((tile, width), BF16)],
        compiler_params=pltpu.CompilerParams(
            dimension_semantics=("arbitrary",), vmem_limit_bytes=VMEM_BYTES
        ),
        cost_estimate=pl.CostEstimate(flops=int(45e9), bytes_accessed=int(50e6), transcendentals=int(4e6)),
    )(length, x, c, att, gp, w1, w2, wo, wqkv, b1, gain1, gain2, shift2)


def shards(
    hidden_in, out_grad, lengths, qkv_weight, qkv_bias, out_weight, out_bias, fc1_weight, fc1_bias,
    fc2_weight, fc2_bias, ln1_gain, ln1_bias, ln2_gain, ln2_bias,
):
    tp_size = lax.axis_size("tp")
    tp_index = lax.axis_index("tp")
    fsdp_index = lax.axis_index("fsdp")
    micro_count, shard_rows, model = hidden_in.shape
    slot = shard_rows * tp_size
    own = out_bias.shape[0]
    cos, sin = rotary_full(slot)
    gather = lambda value, axis: lax.all_gather(value, axis, axis=0, tiled=True)

    small = (qkv_bias, fc1_bias, out_bias, fc2_bias, ln1_gain, ln1_bias, ln2_gain, ln2_bias)
    packed = lax.all_gather(jnp.concatenate(small), "fsdp", axis=0, tiled=False).astype(F32)
    rows, start = [], 0
    for value in small:
        rows.append(packed[:, start:start + value.shape[0]].reshape(1, -1))
        start += value.shape[0]
    bqkv, b1, bo, b2, gain1, shift1, gain2, shift2 = rows
    wqkv = gather(qkv_weight, "fsdp")
    wo = lax.all_gather(out_weight, "fsdp", axis=0, tiled=False)
    w1 = gather(fc1_weight, "fsdp")
    w2 = lax.all_gather(fc2_weight, "fsdp", axis=0, tiled=False)

    parts, outputs, in_grads = [], [], []
    for m in range(micro_count):
        length = lengths[m]
        x = gather(hidden_in[m], "tp")
        c = gather(out_grad[m], "tp")
        n1, att, gp = attention_call(length, x, c, wqkv, bqkv, wo, gain1, shift1, cos, sin)
        n2, act, gpre, h, u, sd, sf, sq = feed_call(
            length, x, c, att, gp, w1, w2, wo, wqkv, b1, gain1, gain2, shift2
        )
        valid = (jnp.arange(slot) < length[0])[:, None]
        cot = jnp.where(valid, c, jnp.zeros_like(c))
        parts.append((n1, att, gp, n2, act, gpre, cot, sd, sf, sq))
        h_own = lax.psum_scatter(h, "tp", scatter_dimension=0, tiled=True)
        u_own = lax.psum_scatter(u, "tp", scatter_dimension=0, tiled=True).astype(F32)
        live = (tp_index * shard_rows + jnp.arange(shard_rows) < length[0])[:, None]
        local = hidden_in[m].astype(F32)
        result = local + h_own.astype(F32) + bo + b2
        outputs.append(jnp.where(live, result, 0.0).astype(BF16))
        xhat, rstd = row_stats(local)
        back = rstd * (
            u_own - jnp.mean(u_own, axis=-1, keepdims=True)
            - xhat * jnp.mean(u_own * xhat, axis=-1, keepdims=True)
        )
        in_grads.append((jnp.where(live, out_grad[m].astype(F32), 0.0) + back).astype(BF16))

    def weight_grad(left, right):
        total = dot_tn(parts[0][left], parts[0][right])
        for part in parts[1:]:
            total = total + dot_tn(part[left], part[right])
        return lax.psum_scatter(total.astype(BF16), "fsdp", scatter_dimension=0, tiled=True).astype(F32)

    grad_up = weight_grad(3, 5)
    grad_down = weight_grad(6, 4).T
    grad_qkv = weight_grad(0, 2)
    grad_out = weight_grad(6, 1).T
    sums = [sum(part[7 + k] for part in parts) for k in range(3)]
    flat = lax.psum(
        jnp.concatenate([sums[0][:5].reshape(-1), sums[1][0], sums[2][0]]), "fsdp"
    )
    wide = 5 * model
    norm = lax.dynamic_slice_in_dim(flat[:wide].reshape(5, model), fsdp_index * own, own, 1)
    ln = lax.psum(norm[:4], "tp")
    own_f, own_q = fc1_bias.shape[0], qkv_bias.shape[0]
    grad_b1 = lax.dynamic_slice_in_dim(flat[wide:wide + w1.shape[1]], fsdp_index * own_f, own_f, 0)
    grad_bq = lax.dynamic_slice_in_dim(flat[wide + w1.shape[1]:], fsdp_index * own_q, own_q, 0)
    return (
        jnp.stack(outputs), jnp.stack(in_grads), grad_qkv, grad_bq, grad_out, norm[4], grad_up, grad_b1,
        grad_down, norm[4], ln[0], ln[1], ln[2], ln[3],
    )


def solution(mesh):
    rows = P(None, ("fsdp", "tp"), None)
    both, column, row, one = P(("tp", "fsdp")), P("fsdp", "tp"), P("tp", "fsdp"), P("fsdp")
    return jax.shard_map(
        shards,
        mesh=mesh,
        in_specs=(rows, rows, P(None, "fsdp"), column, both, row, one, column, both, row, one, one, one, one, one),
        out_specs=(rows, rows, column, both, row, one, column, both, row, one, one, one, one, one),
        check_vma=False,
    )
```

```python
from functools import partial
import math

import jax
import jax.numpy as jnp
from jax import lax
from jax.experimental import pallas as pl
from jax.experimental.pallas import tpu as pltpu
from jax.sharding import PartitionSpec as P

HEAD = 128
ROT = 32
EPSILON = 1e-05
MASKED = -1e30
F32 = jnp.float32
BF16 = jnp.bfloat16
VMEM_BYTES = 60 << 20


def dot_nn(a, b):
    return lax.dot_general(a, b, (((1,), (0,)), ((), ())), preferred_element_type=F32)


def dot_nt(a, b):
    return lax.dot_general(a, b, (((1,), (1,)), ((), ())), preferred_element_type=F32)


def dot_tn(a, b):
    return lax.dot_general(a, b, (((0,), (0,)), ((), ())), preferred_element_type=F32)


def row_stats(rows):
    mean = jnp.mean(rows, axis=-1, keepdims=True)
    centred = rows - mean
    spread = jnp.mean(centred * centred, axis=-1, keepdims=True)
    rstd = lax.rsqrt(spread + EPSILON)
    return centred * rstd, rstd


def rotary_full(row_count):
    half = ROT // 2
    exponent = jnp.arange(0, ROT, 2).astype(F32) / ROT
    inverse = 1.0 / 10000.0**exponent
    angles = jnp.arange(row_count).astype(F32)[:, None] * inverse[None, :]
    cosine, sine = jnp.cos(angles), jnp.sin(angles)
    rest = jnp.ones((row_count, HEAD - ROT), F32)
    return (
        jnp.concatenate([cosine, cosine, rest], axis=1),
        jnp.concatenate([-sine, sine, 0.0 * rest], axis=1),
    )


def swap_halves(block):
    half = ROT // 2
    lane = lax.broadcasted_iota(jnp.int32, block.shape, 1)
    return jnp.where(lane < half, pltpu.roll(block, HEAD - half, 1), pltpu.roll(block, half, 1))

MESH = pl.DeviceIdType.MESH


def greet(axes, lines):
    barrier = pltpu.get_barrier_semaphore()
    count = 0
    for axis, size in axes:
        here = lax.axis_index(axis)
        for k in range(1, size):
            pl.semaphore_signal(
                barrier, inc=1, device_id={axis: lax.rem(here + k, size)}, device_id_type=MESH
            )
        count = count + size - 1
    for axis, size in lines:
        here = lax.axis_index(axis)

        @pl.when(here > 0)
        def _():
            pl.semaphore_signal(barrier, inc=1, device_id={axis: here - 1}, device_id_type=MESH)

        @pl.when(here < size - 1)
        def _():
            pl.semaphore_signal(barrier, inc=1, device_id={axis: here + 1}, device_id_type=MESH)

        count = count + jnp.minimum(here, 1) + jnp.minimum(size - 1 - here, 1)
    pl.semaphore_wait(barrier, count)


class LineGather:
    def __init__(self, size, pieces, src, dst, send, recv, local):
        self.size, self.pieces, self.src, self.dst = size, pieces, src, dst
        self.send, self.recv, self.local = send, recv, local
        self.here = lax.axis_index("tp")
        self.rows = src.shape[0] // pieces

    def copy(self, way, hop, piece, shard, target):
        rows = pl.ds(piece * self.rows, self.rows)
        source = self.src.at[rows] if hop == 0 else self.dst.at[shard, rows]
        return pltpu.make_async_remote_copy(
            source, self.dst.at[shard, rows], self.send.at[way, hop, piece], self.recv.at[way, hop, piece],
            device_id={"tp": target}, device_id_type=MESH,
        )

    def sent(self, way, hop):
        if way == 0:
            return (self.here - hop >= 0) & (self.here < self.size - 1), self.here - hop, self.here + 1
        return (self.here + hop < self.size) & (self.here > 0), self.here + hop, self.here - 1

    def arrived(self, way, hop):
        if way == 0:
            return self.here - 1 - hop >= 0, self.here - 1 - hop
        return self.here + 1 + hop < self.size, self.here + 1 + hop

    def start(self):
        own = pltpu.make_async_copy(self.src, self.dst.at[self.here], self.local)
        own.start()
        for piece in range(self.pieces):
            self.launch(0, piece)

    def launch(self, hop, piece):
        for way in range(2):
            does, shard, target = self.sent(way, hop)

            @pl.when(does)
            def _():
                self.copy(way, hop, piece, shard, target).start()

    def take(self, hop, piece):
        for way in range(2):
            comes, shard = self.arrived(way, hop)

            @pl.when(comes)
            def _():
                self.copy(way, hop, piece, shard, self.here).wait_recv()

    def steps(self):
        def forward(hop, piece):
            self.take(hop - 1, piece)
            self.launch(hop, piece)

        return [partial(forward, hop, piece) for hop in range(1, self.size - 1) for piece in range(self.pieces)]

    def finish(self):
        for piece in range(self.pieces):
            self.take(self.size - 2, piece)
        for hop in range(self.size - 1):
            for piece in range(self.pieces):
                for way in range(2):
                    does, shard, target = self.sent(way, hop)

                    @pl.when(does)
                    def _():
                        self.copy(way, hop, piece, shard, target).wait_send()

        pltpu.make_async_copy(self.src, self.dst.at[self.here], self.local).wait()


def gather_scratch(size, pieces):
    return [
        pltpu.SemaphoreType.DMA((2, size - 1, pieces)), pltpu.SemaphoreType.DMA((2, size - 1, pieces)),
        pltpu.SemaphoreType.DMA,
    ]


def spread(step, slot, slots, total, actions):
    for place in range(total // slots):
        due = [
            act for i, act in enumerate(actions)
            if (i + 1) * total // (len(actions) + 2) == place * slots + slot
        ]
        if due:
            @pl.when(step == place)
            def _():
                for act in due:
                    act()


def first_gather_kernel(size, peers, pieces, x_ref, c_ref, small_ref, xs_ref, cs_ref, smalls_ref, *sems):
    here = lax.axis_index("fsdp")
    greet([("fsdp", peers)], [("tp", size)])
    first = LineGather(size, pieces, x_ref.at[0], xs_ref, *sems[0:3])
    second = LineGather(size, pieces, c_ref.at[0], cs_ref, *sems[3:6])
    small_send, small_recv, small_local = sems[6:9]

    def small_copy(k):
        return pltpu.make_async_remote_copy(
            small_ref, smalls_ref.at[here], small_send.at[k - 1], small_recv.at[k - 1],
            device_id={"fsdp": lax.rem(here + k, peers)}, device_id_type=MESH,
        )

    def small_arrival(k):
        origin = lax.rem(here + peers - k, peers)
        return pltpu.make_async_remote_copy(
            small_ref, smalls_ref.at[origin], small_send.at[k - 1], small_recv.at[k - 1],
            device_id={"fsdp": origin}, device_id_type=MESH,
        )

    first.start()
    second.start()
    own = pltpu.make_async_copy(small_ref, smalls_ref.at[here], small_local)
    own.start()
    for k in range(1, peers):
        small_copy(k).start()
    own.wait()
    for one, two in zip(first.steps(), second.steps()):
        one()
        two()
    first.finish()
    second.finish()
    for k in range(1, peers):
        small_arrival(k).wait_recv()
        small_copy(k).wait_send()


HBM = pl.BlockSpec(memory_space=pltpu.MemorySpace.HBM)


def first_gather(size, peers, x, c, small):
    _, rows, width = x.shape
    pieces = 4
    big = jax.ShapeDtypeStruct((size, rows, width), x.dtype)
    xs, cs, smalls = pl.pallas_call(
        partial(first_gather_kernel, size, peers, pieces),
        in_specs=[HBM] * 3,
        out_specs=[HBM] * 3,
        out_shape=[big, big, jax.ShapeDtypeStruct((peers,) + small.shape, small.dtype)],
        scratch_shapes=gather_scratch(size, pieces) * 2 + [
            pltpu.SemaphoreType.DMA((peers - 1,)), pltpu.SemaphoreType.DMA((peers - 1,)), pltpu.SemaphoreType.DMA,
        ],
        compiler_params=pltpu.CompilerParams(collective_id=0, has_side_effects=True),
        cost_estimate=pl.CostEstimate(flops=0, bytes_accessed=int(500e6), transcendentals=0),
    )(x, c, small)
    return xs.reshape(size * rows, width), cs.reshape(size * rows, width), smalls


def attention_kernel(size, pieces, micro, row_tiles, heads, tile, *refs):
    if micro is None:
        return attention_body(row_tiles, heads, tile, *refs)
    step = pl.program_id(0)
    line = LineGather(size, pieces, refs[10].at[micro], refs[14], *refs[21:])

    @pl.when(step == 0)
    def _():
        greet([], [("tp", size)])
        line.start()

    attention_body(row_tiles, heads, tile, *refs[:10], *refs[11:14], *refs[15:21])
    spread(step, 0, 1, row_tiles + heads, line.steps())

    @pl.when(step == row_tiles + heads - 1)
    def _():
        line.finish()


def attention_body(
    row_tiles, heads, tile, len_ref, x_ref, c_ref, wqkv_ref, bqkv_ref, wo_ref, gain_ref, shift_ref,
    cos_ref, sin_ref, n1_ref, att_ref, gp_ref, q_s, k_s, v_s, ga_s, dk_s, dv_s,
):
    step = pl.program_id(0)
    length = len_ref[0]
    scale = 1.0 / math.sqrt(HEAD)

    @pl.when(step < row_tiles)
    def _():
        rows = pl.ds(pl.multiple_of(step * tile, tile), tile)
        xhat, _ = row_stats(x_ref[...].astype(F32))
        normed = (xhat * gain_ref[...] + shift_ref[...]).astype(BF16)
        n1_ref[...] = normed
        cosine, sine = cos_ref[rows, :], sin_ref[rows, :]
        for h in range(heads):
            part = dot_nn(normed, wqkv_ref[:, h * 384:(h + 1) * 384]) + bqkv_ref[:, h * 384:(h + 1) * 384]
            q, k = part[:, :HEAD], part[:, HEAD:2 * HEAD]
            q_s[h, rows, :] = (q * cosine + swap_halves(q) * sine).astype(BF16)
            k_s[h, rows, :] = (k * cosine + swap_halves(k) * sine).astype(BF16)
            v_s[h, rows, :] = part[:, 2 * HEAD:].astype(BF16)
        place = step * tile + lax.broadcasted_iota(jnp.int32, c_ref.shape, 0)
        cot = jnp.where(place < length, c_ref[...], jnp.zeros_like(c_ref))
        width = wo_ref.shape[2]
        grad = jnp.zeros((tile, heads * HEAD), F32)
        for j in range(wo_ref.shape[0]):
            grad = grad + dot_nt(cot[:, j * width:(j + 1) * width], wo_ref[j])
        for h in range(heads):
            ga_s[h, rows, :] = grad[:, h * HEAD:(h + 1) * HEAD].astype(BF16)

    @pl.when(step >= row_tiles)
    def _():
        h = step - row_tiles
        dk_s[...] = jnp.zeros_like(dk_s)
        dv_s[...] = jnp.zeros_like(dv_s)
        for i in range(row_tiles):
            rows = slice(i * tile, (i + 1) * tile)
            seen = slice(0, (i + 1) * tile)
            q, k, v, ga = q_s[h, rows, :], k_s[h, seen, :], v_s[h, seen, :], ga_s[h, rows, :]
            scores = dot_nt(q, k) * scale
            place = i * tile + lax.broadcasted_iota(jnp.int32, scores.shape, 0)
            key = lax.broadcasted_iota(jnp.int32, scores.shape, 1)
            scores = jnp.where(key <= jnp.minimum(place, length - 1), scores, MASKED)
            top = jnp.max(scores, axis=-1, keepdims=True)
            raised = jnp.exp(scores - top)
            soft = raised * (1.0 / jnp.sum(raised, axis=-1, keepdims=True))
            probs = soft.astype(BF16)
            att_ref[rows, :] = dot_nn(probs, v).astype(BF16)
            grad_probs = dot_nt(ga, v)
            row_dot = jnp.sum(soft * grad_probs, axis=-1, keepdims=True)
            grad_scores = (soft * (grad_probs - row_dot)).astype(BF16)
            dq = dot_nn(grad_scores, k) * scale
            cosine, sine = cos_ref[rows, :], sin_ref[rows, :]
            gp_ref[rows, 0:HEAD] = (dq * cosine - swap_halves(dq) * sine).astype(BF16)
            dk_s[seen, :] += dot_tn(grad_scores, q)
            dv_s[seen, :] += dot_tn(probs, ga)
        dk = dk_s[...] * scale
        gp_ref[:, HEAD:2 * HEAD] = (dk * cos_ref[...] - swap_halves(dk) * sin_ref[...]).astype(BF16)
        gp_ref[:, 2 * HEAD:] = dv_s[...].astype(BF16)


def whole(shape):
    return pl.BlockSpec(shape, lambda i: (0,) * len(shape), pipeline_mode=pl.Buffered(1))


def attention_call(size, length, x, c, wqkv, bqkv, wo, gain, shift, cos, sin, ahead=None, micro=None):
    slot, width = x.shape
    more = micro is not None
    pieces = 2
    gathered = jax.ShapeDtypeStruct((size, slot // size, width), BF16)
    heads = wqkv.shape[1] // (3 * HEAD)
    tile = 256
    row_tiles = slot // tile
    row_block = pl.BlockSpec((tile, width), lambda i: (jnp.minimum(i, row_tiles - 1), 0))
    head_at = lambda i: (0, jnp.maximum(i - row_tiles, 0))
    out = pl.pallas_call(
        partial(attention_kernel, size, pieces, micro, row_tiles, heads, tile),
        grid=(row_tiles + heads,),
        in_specs=[
            pl.BlockSpec(memory_space=pltpu.SMEM), row_block, row_block, whole(wqkv.shape), whole(bqkv.shape),
            whole(wo.shape), whole(gain.shape), whole(shift.shape), whole(cos.shape), whole(sin.shape),
        ] + [HBM] * more,
        out_specs=[
            row_block, pl.BlockSpec((slot, HEAD), head_at), pl.BlockSpec((slot, 3 * HEAD), head_at)
        ] + [HBM] * more,
        out_shape=[
            jax.ShapeDtypeStruct((slot, width), BF16),
            jax.ShapeDtypeStruct((slot, heads * HEAD), BF16),
            jax.ShapeDtypeStruct((slot, heads * 3 * HEAD), BF16),
        ] + [gathered] * more,
        scratch_shapes=[pltpu.VMEM((heads, slot, HEAD), BF16)] * 4 + [pltpu.VMEM((slot, HEAD), F32)] * 2
        + (gather_scratch(size, pieces) if more else []),
        compiler_params=pltpu.CompilerParams(
            dimension_semantics=("arbitrary",), vmem_limit_bytes=VMEM_BYTES,
            **(dict(collective_id=1, has_side_effects=True) if more else {}),
        ),
        cost_estimate=pl.CostEstimate(flops=int(14e9), bytes_accessed=int(20e6), transcendentals=int(3e6)),
    )(length, x, c, wqkv, bqkv, wo, gain, shift, cos, sin, *([ahead] if more else []))
    return (*out[:3], out[3].reshape(slot, width) if more else None)


def normal_pair(value):
    density = jnp.exp(-0.5 * value * value)
    t = 1.0 / (1.0 + (0.3275911 * math.sqrt(0.5)) * jnp.abs(value))
    series = ((((1.061405429 * t - 1.453152027) * t) + 1.421413741) * t - 0.284496736) * t + 0.254829592
    tail = (0.5 * t) * series * density
    return jnp.where(value >= 0, 1.0 - tail, tail), density * (1.0 / math.sqrt(2.0 * math.pi))


def feed_kernel(size, pieces, micro, tile, chunk, steps, *refs):
    if micro is None:
        return feed_body(lambda slot: None, tile, chunk, *refs)
    step = pl.program_id(0)
    line = LineGather(size, pieces, refs[13].at[micro], refs[22], *refs[25:])

    @pl.when(step == 0)
    def _():
        greet([], [("tp", size)])
        line.start()

    feed_body(
        lambda slot: spread(step, slot, 4, 4 * steps, line.steps()), tile, chunk, *refs[:13], *refs[14:22], *refs[23:25]
    )

    @pl.when(step == steps - 1)
    def _():
        line.finish()


def feed_body(
    hook, tile, chunk, len_ref, x_ref, c_ref, att_ref, gp_ref, w1_ref, w2_ref, wo_ref, wqkv_ref, b1_ref,
    gain1_ref, gain2_ref, shift2_ref, n2_ref, act_ref, gpre_ref, h_ref, u_ref, sd_ref, sf_ref, sq_ref, xhat_s, cot_s,
):
    step = pl.program_id(0)
    length = len_ref[0]
    blocks, hidden, width = w2_ref.shape
    model = x_ref.shape[1]

    @pl.when(step == 0)
    def _():
        sd_ref[...] = jnp.zeros_like(sd_ref)
        sf_ref[...] = jnp.zeros_like(sf_ref)
        sq_ref[...] = jnp.zeros_like(sq_ref)

    xhat, _ = row_stats(x_ref[...].astype(F32))
    xhat_s[...] = xhat
    n2_ref[...] = (xhat * gain2_ref[...] + shift2_ref[...]).astype(BF16)
    place = step * tile + lax.broadcasted_iota(jnp.int32, c_ref.shape, 0)
    cot_s[...] = jnp.where(place < length, c_ref[...], jnp.zeros_like(c_ref))
    ones = jnp.ones((8, tile), BF16)
    for k in range(hidden // chunk):
        cols = slice(k * chunk, (k + 1) * chunk)
        pre = dot_nn(n2_ref[...], w1_ref[:, cols]) + b1_ref[:, cols]
        below, density = normal_pair(pre)
        act_ref[:, cols] = (pre * below).astype(BF16)
        gact = dot_nt(cot_s[:, 0:width], w2_ref[0, cols, :])
        for j in range(1, blocks):
            gact = gact + dot_nt(cot_s[:, j * width:(j + 1) * width], w2_ref[j, cols, :])
        gpre = (gact * (below + pre * density)).astype(BF16)
        gpre_ref[:, cols] = gpre
        sf_ref[:, cols] += dot_nn(ones, gpre)
        if k == hidden // chunk // 2 - 1:
            hook(0)
    hook(1)
    sq_ref[...] += dot_nn(ones, gp_ref[...])
    for j in range(blocks):
        cols = slice(j * width, (j + 1) * width)
        h_ref[:, cols] = (dot_nn(act_ref[...], w2_ref[j]) + dot_nn(att_ref[...], wo_ref[j])).astype(BF16)
    hook(2)
    for k in range(model // chunk):
        cols = slice(k * chunk, (k + 1) * chunk)
        g2 = dot_nt(gpre_ref[...], w1_ref[cols, :])
        g1 = dot_nt(gp_ref[...], wqkv_ref[cols, :])
        u_ref[:, cols] = (g1 * gain1_ref[:, cols] + g2 * gain2_ref[:, cols]).astype(BF16)
        hat = xhat_s[:, cols]
        sd_ref[0:1, cols] += jnp.sum(g1 * hat, axis=0, keepdims=True)
        sd_ref[1:2, cols] += jnp.sum(g1, axis=0, keepdims=True)
        sd_ref[2:3, cols] += jnp.sum(g2 * hat, axis=0, keepdims=True)
        sd_ref[3:4, cols] += jnp.sum(g2, axis=0, keepdims=True)
        sd_ref[4:5, cols] += dot_nn(ones, cot_s[:, cols])[0:1]
    hook(3)


def feed_call(size, length, x, c, att, gp, w1, w2, wo, wqkv, b1, gain1, gain2, shift2, ahead=None, micro=None):
    slot, width = x.shape
    more = micro is not None
    pieces = 2
    gathered = jax.ShapeDtypeStruct((size, slot // size, width), BF16)
    hidden = w1.shape[1]
    tile, chunk = 256, 512
    at = lambda i: (i, 0)
    keep = lambda i: (0, 0)
    row_block = pl.BlockSpec((tile, width), at)
    hid_block = pl.BlockSpec((tile, hidden), at)
    out = pl.pallas_call(
        partial(feed_kernel, size, pieces, micro, tile, chunk, slot // tile),
        grid=(slot // tile,),
        in_specs=[
            pl.BlockSpec(memory_space=pltpu.SMEM), row_block, row_block, pl.BlockSpec((tile, att.shape[1]), at),
            pl.BlockSpec((tile, gp.shape[1]), at), whole(w1.shape), whole(w2.shape), whole(wo.shape),
            whole(wqkv.shape), whole(b1.shape), whole(gain1.shape), whole(gain2.shape), whole(shift2.shape),
        ] + [HBM] * more,
        out_specs=[
            row_block, hid_block, hid_block, row_block, row_block,
            pl.BlockSpec((8, width), keep), pl.BlockSpec((8, hidden), keep), pl.BlockSpec((8, gp.shape[1]), keep),
        ] + [HBM] * more,
        out_shape=[
            jax.ShapeDtypeStruct((slot, width), BF16),
            jax.ShapeDtypeStruct((slot, hidden), BF16),
            jax.ShapeDtypeStruct((slot, hidden), BF16),
            jax.ShapeDtypeStruct((slot, width), BF16),
            jax.ShapeDtypeStruct((slot, width), BF16),
            jax.ShapeDtypeStruct((8, width), F32),
            jax.ShapeDtypeStruct((8, hidden), F32),
            jax.ShapeDtypeStruct((8, gp.shape[1]), F32),
        ] + [gathered] * more,
        scratch_shapes=[pltpu.VMEM((tile, width), F32), pltpu.VMEM((tile, width), BF16)]
        + (gather_scratch(size, pieces) if more else []),
        compiler_params=pltpu.CompilerParams(
            dimension_semantics=("arbitrary",), vmem_limit_bytes=VMEM_BYTES,
            **(dict(collective_id=2, has_side_effects=True) if more else {}),
        ),
        cost_estimate=pl.CostEstimate(flops=int(45e9), bytes_accessed=int(50e6), transcendentals=int(4e6)),
    )(length, x, c, att, gp, w1, w2, wo, wqkv, b1, gain1, gain2, shift2, *([ahead] if more else []))
    return (*out[:8], out[8].reshape(slot, width) if more else None)


def shards(
    hidden_in, out_grad, lengths, qkv_weight, qkv_bias, out_weight, out_bias, fc1_weight, fc1_bias,
    fc2_weight, fc2_bias, ln1_gain, ln1_bias, ln2_gain, ln2_bias,
):
    tp_size = lax.axis_size("tp")
    tp_index = lax.axis_index("tp")
    fsdp_index = lax.axis_index("fsdp")
    micro_count, shard_rows, model = hidden_in.shape
    slot = shard_rows * tp_size
    own = out_bias.shape[0]
    cos, sin = rotary_full(slot)
    gather = lambda value, axis: lax.all_gather(value, axis, axis=0, tiled=True)

    small = (qkv_bias, fc1_bias, out_bias, fc2_bias, ln1_gain, ln1_bias, ln2_gain, ln2_bias)
    flat = jnp.concatenate(small).astype(F32)
    lines = 8 * 128
    flat = jnp.pad(flat, (0, -flat.shape[0] % lines)).reshape(8, -1)
    peers = lax.axis_size("fsdp")
    x, c, packed = first_gather(tp_size, peers, hidden_in, out_grad, flat)
    packed = packed.reshape(peers, -1)
    rows, start = [], 0
    for value in small:
        rows.append(packed[:, start:start + value.shape[0]].reshape(1, -1))
        start += value.shape[0]
    bqkv, b1, bo, b2, gain1, shift1, gain2, shift2 = rows
    wqkv = gather(qkv_weight, "fsdp")
    wo = lax.all_gather(out_weight, "fsdp", axis=0, tiled=False)
    w1 = gather(fc1_weight, "fsdp")
    w2 = lax.all_gather(fc2_weight, "fsdp", axis=0, tiled=False)

    parts, outputs, in_grads = [], [], []
    for m in range(micro_count):
        length = lengths[m]
        ahead = dict(ahead=hidden_in, micro=m + 1) if m + 1 < micro_count else {}
        n1, att, gp, x_next = attention_call(
            tp_size, length, x, c, wqkv, bqkv, wo, gain1, shift1, cos, sin, **ahead
        )
        ahead = dict(ahead=out_grad, micro=m + 1) if m + 1 < micro_count else {}
        n2, act, gpre, h, u, sd, sf, sq, c_next = feed_call(
            tp_size, length, x, c, att, gp, w1, w2, wo, wqkv, b1, gain1, gain2, shift2, **ahead
        )
        valid = (jnp.arange(slot) < length[0])[:, None]
        cot = jnp.where(valid, c, jnp.zeros_like(c))
        parts.append((n1, att, gp, n2, act, gpre, cot, sd, sf, sq))
        h_own = lax.psum_scatter(h, "tp", scatter_dimension=0, tiled=True)
        u_own = lax.psum_scatter(u, "tp", scatter_dimension=0, tiled=True).astype(F32)
        live = (tp_index * shard_rows + jnp.arange(shard_rows) < length[0])[:, None]
        local = hidden_in[m].astype(F32)
        result = local + h_own.astype(F32) + bo + b2
        outputs.append(jnp.where(live, result, 0.0).astype(BF16))
        xhat, rstd = row_stats(local)
        back = rstd * (
            u_own - jnp.mean(u_own, axis=-1, keepdims=True)
            - xhat * jnp.mean(u_own * xhat, axis=-1, keepdims=True)
        )
        in_grads.append((jnp.where(live, out_grad[m].astype(F32), 0.0) + back).astype(BF16))
        x, c = x_next, c_next

    def weight_grad(left, right):
        total = dot_tn(parts[0][left], parts[0][right])
        for part in parts[1:]:
            total = total + dot_tn(part[left], part[right])
        return lax.psum_scatter(total.astype(BF16), "fsdp", scatter_dimension=0, tiled=True).astype(F32)

    grad_up = weight_grad(3, 5)
    grad_down = weight_grad(6, 4).T
    grad_qkv = weight_grad(0, 2)
    grad_out = weight_grad(6, 1).T
    sums = [sum(part[7 + k] for part in parts) for k in range(3)]
    flat = lax.psum(
        jnp.concatenate([sums[0][:5].reshape(-1), sums[1][0], sums[2][0]]), "fsdp"
    )
    wide = 5 * model
    norm = lax.dynamic_slice_in_dim(flat[:wide].reshape(5, model), fsdp_index * own, own, 1)
    ln = lax.psum(norm[:4], "tp")
    own_f, own_q = fc1_bias.shape[0], qkv_bias.shape[0]
    grad_b1 = lax.dynamic_slice_in_dim(flat[wide:wide + w1.shape[1]], fsdp_index * own_f, own_f, 0)
    grad_bq = lax.dynamic_slice_in_dim(flat[wide + w1.shape[1]:], fsdp_index * own_q, own_q, 0)
    return (
        jnp.stack(outputs), jnp.stack(in_grads), grad_qkv, grad_bq, grad_out, norm[4], grad_up, grad_b1,
        grad_down, norm[4], ln[0], ln[1], ln[2], ln[3],
    )


def solution(mesh):
    rows = P(None, ("fsdp", "tp"), None)
    both, column, row, one = P(("tp", "fsdp")), P("fsdp", "tp"), P("tp", "fsdp"), P("fsdp")
    return jax.shard_map(
        shards,
        mesh=mesh,
        in_specs=(rows, rows, P(None, "fsdp"), column, both, row, one, column, both, row, one, one, one, one, one),
        out_specs=(rows, rows, column, both, row, one, column, both, row, one, one, one, one, one),
        check_vma=False,
    )
```

```python
from functools import partial
import math

import jax
import jax.numpy as jnp
import numpy as np
from jax import lax
from jax.experimental import pallas as pl
from jax.experimental.pallas import tpu as pltpu
from jax.sharding import PartitionSpec as P

HEAD = 128
ROT = 32
EPSILON = 1e-05
MASKED = -1e30
F32 = jnp.float32
BF16 = jnp.bfloat16
VMEM_BYTES = 60 << 20


def dot_nn(a, b):
    return lax.dot_general(a, b, (((1,), (0,)), ((), ())), preferred_element_type=F32)


def dot_nt(a, b):
    return lax.dot_general(a, b, (((1,), (1,)), ((), ())), preferred_element_type=F32)


def dot_tn(a, b):
    return lax.dot_general(a, b, (((0,), (0,)), ((), ())), preferred_element_type=F32)


def row_stats(rows):
    mean = jnp.mean(rows, axis=-1, keepdims=True)
    centred = rows - mean
    spread = jnp.mean(centred * centred, axis=-1, keepdims=True)
    rstd = lax.rsqrt(spread + EPSILON)
    return centred * rstd, rstd


def rotary_full(row_count):
    exponent = np.arange(0, ROT, 2, dtype=np.float32) / np.float32(ROT)
    inverse = (1.0 / 10000.0 ** exponent.astype(np.float64)).astype(np.float32)
    angles = (np.arange(row_count, dtype=np.float32)[:, None] * inverse[None, :]).astype(np.float64)
    cosine, sine = np.cos(angles).astype(np.float32), np.sin(angles).astype(np.float32)
    rest = np.ones((row_count, HEAD - ROT), np.float32)
    return (
        jnp.asarray(np.concatenate([cosine, cosine, rest], axis=1)),
        jnp.asarray(np.concatenate([-sine, sine, 0.0 * rest], axis=1)),
    )


def swap_halves(block):
    half = ROT // 2
    lane = lax.broadcasted_iota(jnp.int32, block.shape, 1)
    return jnp.where(lane < half, pltpu.roll(block, HEAD - half, 1), pltpu.roll(block, half, 1))

MESH = pl.DeviceIdType.MESH


def greet(axes, lines):
    barrier = pltpu.get_barrier_semaphore()
    count = 0
    for axis, size in axes:
        here = lax.axis_index(axis)
        for k in range(1, size):
            pl.semaphore_signal(
                barrier, inc=1, device_id={axis: lax.rem(here + k, size)}, device_id_type=MESH
            )
        count = count + size - 1
    for axis, size in lines:
        here = lax.axis_index(axis)

        @pl.when(here > 0)
        def _():
            pl.semaphore_signal(barrier, inc=1, device_id={axis: here - 1}, device_id_type=MESH)

        @pl.when(here < size - 1)
        def _():
            pl.semaphore_signal(barrier, inc=1, device_id={axis: here + 1}, device_id_type=MESH)

        count = count + jnp.minimum(here, 1) + jnp.minimum(size - 1 - here, 1)
    pl.semaphore_wait(barrier, count)


class LineGather:
    def __init__(self, size, pieces, src, dst, send, recv, local):
        self.size, self.pieces, self.src, self.dst = size, pieces, src, dst
        self.send, self.recv, self.local = send, recv, local
        self.here = lax.axis_index("tp")
        self.rows = src.shape[0] // pieces
        self.settled = False

    def copy(self, way, hop, piece, shard, target):
        rows = pl.ds(piece * self.rows, self.rows)
        source = self.src.at[rows] if hop == 0 else self.dst.at[shard, rows]
        return pltpu.make_async_remote_copy(
            source, self.dst.at[shard, rows], self.send.at[way, hop, piece], self.recv.at[way, hop, piece],
            device_id={"tp": target}, device_id_type=MESH,
        )

    def sent(self, way, hop):
        if way == 0:
            return (self.here - hop >= 0) & (self.here < self.size - 1), self.here - hop, self.here + 1
        return (self.here + hop < self.size) & (self.here > 0), self.here + hop, self.here - 1

    def arrived(self, way, hop):
        if way == 0:
            return self.here - 1 - hop >= 0, self.here - 1 - hop
        return self.here + 1 + hop < self.size, self.here + 1 + hop

    def start(self):
        own = pltpu.make_async_copy(self.src, self.dst.at[self.here], self.local)
        own.start()
        for piece in range(self.pieces):
            self.launch(0, piece)

    def launch(self, hop, piece):
        for way in range(2):
            does, shard, target = self.sent(way, hop)

            @pl.when(does)
            def _():
                self.copy(way, hop, piece, shard, target).start()

    def take(self, hop, piece):
        for way in range(2):
            comes, shard = self.arrived(way, hop)

            @pl.when(comes)
            def _():
                self.copy(way, hop, piece, shard, self.here).wait_recv()

    def steps(self):
        def forward(hop, piece):
            self.take(hop - 1, piece)
            self.launch(hop, piece)

        return [partial(forward, hop, piece) for hop in range(1, self.size - 1) for piece in range(self.pieces)]

    def finish(self, taken=False):
        if not taken:
            for piece in range(self.pieces):
                self.take(self.size - 2, piece)
        for hop in range(self.size - 1):
            for piece in range(self.pieces):
                for way in range(2):
                    does, shard, target = self.sent(way, hop)

                    @pl.when(does)
                    def _():
                        self.copy(way, hop, piece, shard, target).wait_send()

        if not self.settled:
            self.settle()

    def settle(self):
        self.settled = True
        pltpu.make_async_copy(self.src, self.dst.at[self.here], self.local).wait()

    def order(self, j):
        both = jnp.minimum(self.here, self.size - 1 - self.here)
        near = self.here + jnp.where(lax.rem(j, 2) == 0, j // 2, -((j + 1) // 2))
        rest = jnp.where(self.here < self.size - 1 - self.here, j, self.size - 1 - j)
        return jnp.where(j <= 2 * both, near, rest)


def gather_scratch(size, pieces):
    return [
        pltpu.SemaphoreType.DMA((2, size - 1, pieces)), pltpu.SemaphoreType.DMA((2, size - 1, pieces)),
        pltpu.SemaphoreType.DMA,
    ]


class PlaneGather:
    def __init__(self, peers, src, dst, send, recv, pass_send, pass_recv, local):
        self.chips, self.src, self.dst = peers // 2, src, dst
        self.send, self.recv, self.pass_send, self.pass_recv, self.local = send, recv, pass_send, pass_recv, local
        self.here = lax.axis_index("fsdp")
        self.chip, self.core = self.here // 2, lax.rem(self.here, 2)

    def far(self, s, origin):
        return pltpu.make_async_remote_copy(
            self.src, self.dst.at[origin], self.send.at[s], self.recv.at[s],
            device_id={"fsdp": 2 * lax.rem(self.chip + s, self.chips) + self.core}, device_id_type=MESH,
        )

    def origin(self, s, core):
        return 2 * lax.rem(self.chip + self.chips - s, self.chips) + core

    def near(self, s, core):
        shard = self.origin(s, core)
        return pltpu.make_async_remote_copy(
            self.src if s == 0 else self.dst.at[shard], self.dst.at[shard], self.pass_send.at[s], self.pass_recv.at[s],
            device_id={"fsdp": 2 * self.chip + 1 - self.core}, device_id_type=MESH,
        )

    def start(self):
        pltpu.make_async_copy(self.src, self.dst.at[self.here], self.local).start()
        for s in range(1, self.chips):
            self.far(s, self.here).start()
        self.near(0, self.core).start()

    def steps(self):
        def forward(s):
            self.far(s, self.origin(s, self.core)).wait_recv()
            self.near(s, self.core).start()

        return [partial(forward, s) for s in range(1, self.chips)]

    def finish(self):
        for s in range(self.chips):
            self.near(s, 1 - self.core).wait_recv()
            self.near(s, self.core).wait_send()
            if s:
                self.far(s, self.here).wait_send()
        pltpu.make_async_copy(self.src, self.dst.at[self.here], self.local).wait()


class LineReduce:
    def __init__(self, size, pieces, part, held, last, term, send, recv, load):
        self.size, self.pieces, self.part, self.held, self.last = size, pieces, part, held, last
        self.term, self.send, self.recv, self.load = term, send, recv, load
        self.here = lax.axis_index("tp")
        self.rows = part.shape[1] // pieces
        self.place = (self.here, size - 1 - self.here)

    def span(self, piece):
        return pl.ds(piece * self.rows, self.rows)

    def shard(self, way, hop):
        far = self.size + self.place[way] - hop
        return far if way == 0 else self.size - 1 - far

    def copy(self, way, hop, piece, first):
        rows = self.span(piece)
        source = self.part.at[self.shard(way, hop), rows] if first else self.held.at[way, hop - 2, rows]
        goal = self.last.at[way, rows] if hop == self.size - 1 else self.held.at[way, hop - 1, rows]
        return pltpu.make_async_remote_copy(
            source, goal, self.send.at[way, hop - 1, piece], self.recv.at[way, hop - 1, piece],
            device_id={"tp": self.here + (1 if way == 0 else -1)}, device_id_type=MESH,
        )

    def arrival(self, way, hop, piece):
        rows = self.span(piece)
        goal = self.last.at[way, rows] if hop == self.size - 1 else self.held.at[way, hop - 1, rows]
        return pltpu.make_async_remote_copy(
            self.part.at[0, rows], goal, self.send.at[way, hop - 1, piece], self.recv.at[way, hop - 1, piece],
            device_id={"tp": self.here}, device_id_type=MESH,
        )

    def own(self, way, hop, piece):
        return pltpu.make_async_copy(
            self.part.at[self.shard(way, hop), self.span(piece)], self.term.at[way], self.load.at[way]
        )

    def begin(self, hop, piece):
        for way in range(2):
            @pl.when(self.place[way] == 0)
            def _():
                if hop > 1:
                    self.copy(way, hop - 1, piece, True).wait_send()
                self.copy(way, hop, piece, True).start()

    def start(self):
        for piece in range(self.pieces):
            self.begin(1, piece)

    def forward(self, hop, piece):
        passes = [
            (self.place[way] > 0) & (self.place[way] < hop) & (self.place[way] < self.size - 1) for way in range(2)
        ]
        for way in range(2):
            @pl.when(passes[way])
            def _():
                self.own(way, hop, piece).start()

        self.begin(hop, piece)
        for way in range(2):
            @pl.when(passes[way])
            def _():
                self.arrival(way, hop - 1, piece).wait_recv()
                self.own(way, hop, piece).wait()
                rows = self.span(piece)
                total = self.held[way, hop - 2, rows].astype(F32) + self.term[way].astype(F32)
                self.held[way, hop - 2, rows] = total.astype(BF16)
                self.copy(way, hop, piece, False).start()

    def steps(self):
        return [
            partial(self.forward, hop, piece) for hop in range(2, self.size) for piece in range(self.pieces)
        ]

    def finish(self):
        for piece in range(self.pieces):
            for way in range(2):
                @pl.when(self.place[way] > 0)
                def _():
                    self.arrival(way, self.size - 1, piece).wait_recv()

        for hop in range(1, self.size):
            for piece in range(self.pieces):
                for way in range(2):
                    late = self.place[way] > 0 if hop < self.size - 1 else True

                    @pl.when((self.place[way] < hop) & (self.place[way] < self.size - 1) & late)
                    def _():
                        self.copy(way, hop, piece, True).wait_send()


def reduce_scratch(size, pieces, rows, width):
    dma = pltpu.SemaphoreType.DMA
    return [
        pltpu.VMEM((2, size - 2, rows, width), BF16), pltpu.VMEM((2, rows // pieces, width), BF16),
        dma((2, size - 1, pieces)), dma((2, size - 1, pieces)), dma((2,)),
    ]


class Job:
    def __init__(self, inputs, outputs, scratch, build):
        self.inputs, self.outputs, self.scratch, self.build = inputs, outputs, scratch, build


def gather_job(size, pieces, array, micro):
    _, rows, width = array.shape
    return Job(
        [array], [jax.ShapeDtypeStruct((size, rows, width), array.dtype)], gather_scratch(size, pieces),
        lambda ins, outs, scratch: LineGather(size, pieces, ins[0].at[micro], outs[0], *scratch),
    )


def landing_job(size, pieces, array, micro):
    _, rows, width = array.shape
    big = (size, rows, width)
    return Job(
        [array], [jax.ShapeDtypeStruct(big, array.dtype)], gather_scratch(size, pieces) + [
            pltpu.VMEM(big, array.dtype), pltpu.SemaphoreType.DMA((size,))
        ],
        lambda ins, outs, scratch: LineGather(size, pieces, ins[0].at[micro], scratch[3], *scratch[:3]),
    )


def reduce_job(size, pieces, side):
    slot, width = side.shape
    rows = slot // size
    return Job(
        [side.reshape(size, rows, width)], [jax.ShapeDtypeStruct((2, rows, width), BF16)],
        reduce_scratch(size, pieces, rows, width),
        lambda ins, outs, scratch: LineReduce(size, pieces, ins[0], *scratch[:1], outs[0], *scratch[1:]),
    )


def with_jobs(jobs, counts, refs):
    refs = list(refs)
    own, theirs = [], []
    for count, kind in zip(counts, ("inputs", "outputs", "scratch")):
        own += refs[:count]
        del refs[:count]
        theirs.append([])
        for job in jobs:
            many = len(getattr(job, kind))
            theirs[-1].append(refs[:many])
            del refs[:many]
    return own, [job.build(*parts) for job, parts in zip(jobs, zip(*theirs))], list(zip(*theirs))


def job_lists(jobs):
    return (
        [x for job in jobs for x in job.inputs], [x for job in jobs for x in job.outputs],
        [x for job in jobs for x in job.scratch],
    )


def spread(step, slot, slots, total, actions):
    for place in range(total // slots):
        due = [
            act for i, act in enumerate(actions)
            if (i + 1) * total // (len(actions) + 2) == place * slots + slot
        ]
        if due:
            @pl.when(step == place)
            def _():
                for act in due:
                    act()


HBM = pl.BlockSpec(memory_space=pltpu.MemorySpace.HBM)


def attention_kernel(size, jobs, row_tiles, heads, tile, *refs):
    own, lines, parts = with_jobs(jobs, (9, 3, 11), refs)
    (len_ref, x_ref, wqkv_hbm, bqkv_ref, wo_hbm, gain_ref, shift_ref, cos_ref, sin_ref, *rest) = own
    wqkv_s, wo_s, w_sem, wo_sem = rest[-4:]

    def begin():
        load_qkv = pltpu.make_async_copy(wqkv_hbm, wqkv_s, w_sem.at[0])
        load_qkv.start()
        greet([], [("tp", size)])
        for line in lines:
            line.start()
        for copy in side_by_side(wo_hbm, wo_s, wo_sem):
            copy.start()
        load_qkv.wait()

    attention_body(
        size, lines, parts, row_tiles, heads, tile, 0, begin, lambda: x_ref[...],
        lambda: [copy.wait() for copy in side_by_side(wo_hbm, wo_s, wo_sem)],
        len_ref, bqkv_ref, gain_ref, shift_ref, cos_ref, sin_ref, *rest[:-2],
    )


def opening_kernel(size, peers, pieces, counts, jobs, row_tiles, heads, tile, *refs):
    many = len(counts)
    own, lines, parts = with_jobs(jobs, (6 + many, 6 + many, 11 + 2 + 17), refs)
    len_ref, x_ref, wa_ref, wb_ref, cos_ref, sin_ref = own[:6]
    smalls, own = own[6:6 + many], own[6 + many:]
    n1_ref, att_ref, gp_ref, xs_ref, was_ref, wbs_ref = own[:6]
    outs, own = own[6:6 + many], own[6 + many:]
    work, (x_s, x_sem), more = own[:11], own[11:13], own[13:]
    send, recv, local, pack, packs, small_send, small_recv, *plane = more
    wqkv_s, wo_s, w_sem, wo_sem = work[-4:]
    here = lax.axis_index("fsdp")
    shard = xs_ref.shape[1]
    share = tile // shard

    def load_rows(at):
        slot = lax.rem(at, 2)
        return [
            pltpu.make_async_copy(
                xs_ref.at[at * share + k], x_s.at[slot, pl.ds(k * shard, shard)], x_sem.at[slot, k]
            ) for k in range(share)
        ]

    def small_copy(k, origin):
        return pltpu.make_async_remote_copy(
            pack, packs.at[origin], small_send.at[k - 1], small_recv.at[k - 1],
            device_id={"fsdp": lax.rem(here + k, peers)}, device_id_type=MESH,
        )

    def begin():
        greet([("fsdp", peers)], [("tp", size)])
        line = LineGather(size, pieces, x_ref.at[0], xs_ref, send, recv, local)
        line.start()
        weights = [PlaneGather(peers, wa_ref, was_ref, *plane[:5]), PlaneGather(peers, wb_ref, wbs_ref, *plane[5:])]
        for row, (small, count) in enumerate(zip(smalls, counts)):
            pack[row:row + 1, 0:count] = small[...].astype(F32).reshape(1, count)
        for k in range(1, peers):
            small_copy(k, here).start()
        packs[here] = pack[...]
        for weight in weights:
            weight.start()
        for act in line.steps():
            act()
        for one in lines:
            one.start()
        for weight in weights:
            for act in weight.steps():
                act()
        for k in range(1, peers):
            small_copy(k, lax.rem(here + peers - k, peers)).wait_recv()
            small_copy(k, here).wait_send()
        for row, (out, count) in enumerate(zip(outs, counts)):
            for peer in range(peers):
                out[0:1, peer * count:(peer + 1) * count] = packs[peer, row:row + 1, 0:count]
        for weight in weights:
            weight.finish()
        rows = wa_ref.shape[0]
        loads = [
            pltpu.make_async_copy(was_ref.at[k], wqkv_s.at[pl.ds(k * rows, rows)], w_sem.at[k]) for k in range(peers)
        ]
        for copy in loads + side_by_side(wbs_ref, wo_s, wo_sem):
            copy.start()
        line.finish()
        for act in lines[0].steps()[:lines[0].pieces]:
            act()
        for copy in load_rows(0):
            copy.start()
        for copy in loads:
            copy.wait()

    def rows_now():
        step = pl.program_id(0)

        @pl.when(step + 1 < row_tiles)
        def _():
            for copy in load_rows(step + 1):
                copy.start()

        for copy in load_rows(step):
            copy.wait()
        return x_s[lax.rem(step, 2)]

    attention_body(
        size, lines, parts, row_tiles, heads, tile, 1, begin, rows_now,
        lambda: [copy.wait() for copy in side_by_side(wbs_ref, wo_s, wo_sem)],
        len_ref, outs[0], outs[4], outs[5], cos_ref, sin_ref, n1_ref, att_ref, gp_ref, *work[:-2],
    )


def attention_body(
    size, lines, parts, row_tiles, heads, tile, ahead, begin, rows_now, out_ready, len_ref, bqkv_ref, gain_ref, shift_ref,
    cos_ref, sin_ref, n1_ref, att_ref, gp_ref, q_s, k_s, v_s, ga_s, p_s, dk_s, dv_s, wqkv_ref, wo_ref,
):
    cot, landed, out_sem = lines[0], parts[0][2][3], parts[0][2][4]

    def publish(shard):
        return pltpu.make_async_copy(landed.at[shard], parts[0][1][0].at[shard], out_sem.at[shard])

    step = pl.program_id(0)
    length = len_ref[0]
    scale = 1.0 / math.sqrt(HEAD)

    @pl.when(step == 0)
    def _():
        dk_s[...] = jnp.zeros_like(dk_s)
        dv_s[...] = jnp.zeros_like(dv_s)
        begin()

    @pl.when(step < row_tiles)
    def _():
        rows = pl.ds(pl.multiple_of(step * tile, tile), tile)
        xhat, _ = row_stats(rows_now().astype(F32))
        normed = (xhat * gain_ref[...] + shift_ref[...]).astype(BF16)
        n1_ref[...] = normed
        cosine, sine = cos_ref[rows, :], sin_ref[rows, :]
        for h in range(heads):
            part = dot_nn(normed, wqkv_ref[:, h * 384:(h + 1) * 384]) + bqkv_ref[:, h * 384:(h + 1) * 384]
            q, k = part[:, :HEAD], part[:, HEAD:2 * HEAD]
            q_s[h, rows, :] = (q * cosine + swap_halves(q) * sine).astype(BF16)
            k_s[h, rows, :] = (k * cosine + swap_halves(k) * sine).astype(BF16)
            v_s[h, rows, :] = part[:, 2 * HEAD:].astype(BF16)

    @pl.when((step >= row_tiles) & (step < row_tiles + heads))
    def _():
        h = step - row_tiles
        for i in range(row_tiles):
            rows, seen = slice(i * tile, (i + 1) * tile), slice(0, (i + 1) * tile)
            scores = dot_nt(q_s[h, rows, :], k_s[h, seen, :]) * scale
            place = i * tile + lax.broadcasted_iota(jnp.int32, scores.shape, 0)
            key = lax.broadcasted_iota(jnp.int32, scores.shape, 1)
            scores = jnp.where(key <= jnp.minimum(place, length - 1), scores, MASKED)
            top = jnp.max(scores, axis=-1, keepdims=True)
            raised = jnp.exp(scores - top)
            probs = (raised * (1.0 / jnp.sum(raised, axis=-1, keepdims=True))).astype(BF16)
            p_s[h, rows, seen] = probs
            att_ref[rows, :] = dot_nn(probs, v_s[h, seen, :]).astype(BF16)

    @pl.when(step == row_tiles + heads)
    def _():
        shard = landed.shape[1]
        out_ready()

        def block_back(c, h, ga):
            rows, seen = slice(c * shard, (c + 1) * shard), slice(0, (c + 1) * shard)
            probs = p_s[h, rows, seen]
            soft = probs.astype(F32)
            grad_probs = dot_nt(ga, v_s[h, seen, :])
            row_dot = jnp.sum(soft * grad_probs, axis=-1, keepdims=True)
            grad_scores = (soft * (grad_probs - row_dot)).astype(BF16)
            dq = dot_nn(grad_scores, k_s[h, seen, :]) * scale
            cosine, sine = cos_ref[rows, :], sin_ref[rows, :]
            gp_ref[rows, pl.ds(pl.multiple_of(h * 3 * HEAD, HEAD), HEAD)] = (
                dq * cosine - swap_halves(dq) * sine
            ).astype(BF16)
            dk_s[h, seen, :] += dot_tn(grad_scores, q_s[h, rows, :])
            dv_s[h, seen, :] += dot_tn(probs, ga)

        def arrive(j):
            if j == 0:
                cot.settle()
            elif j < size - 1:
                for act in cot.steps()[(j - 1) * cot.pieces:j * cot.pieces] if j > ahead else []:
                    act()
            else:
                for piece in range(cot.pieces):
                    cot.take(size - 2, piece)
            for line in lines[1:]:
                if 1 <= j < size - 1:
                    for act in line.steps()[(j - 1) * line.pieces:j * line.pieces]:
                        act()

        def one_shard(j, carry):
            for k in range(size):
                @pl.when(j == k)
                def _():
                    arrive(k)
            at = cot.order(j)
            place = at * shard + lax.broadcasted_iota(jnp.int32, landed.shape[1:], 0)
            publish(at).start()
            block = landed[at]
            ga_s[...] = dot_nt(jnp.where(place < length, block, jnp.zeros_like(block)), wo_ref[...]).astype(BF16)
            for c in range(size):
                @pl.when(at == c)
                def _():
                    def one(h, carry):
                        block_back(c, h, ga_s[:, pl.ds(pl.multiple_of(h * HEAD, HEAD), HEAD)])
                        return carry

                    lax.fori_loop(0, heads, one, 0)
            return carry

        lax.fori_loop(0, size, one_shard, 0)
        def close_head(h, carry):
            first = pl.multiple_of(h * 3 * HEAD, HEAD)
            dk = dk_s[h] * scale
            gp_ref[:, pl.ds(first + HEAD, HEAD)] = (
                dk * cos_ref[...] - swap_halves(dk) * sin_ref[...]
            ).astype(BF16)
            gp_ref[:, pl.ds(first + 2 * HEAD, HEAD)] = dv_s[h].astype(BF16)
            return carry

        lax.fori_loop(0, heads, close_head, 0)
        cot.finish(taken=True)
        for line in lines[1:]:
            line.finish()
        for k in range(size):
            publish(k).wait()


def side_by_side(parts, goal, sem):
    peers, _, width = parts.shape
    return [
        pltpu.make_async_copy(parts.at[j], goal.at[:, pl.ds(j * width, width)], sem.at[j]) for j in range(peers)
    ]


def whole(shape):
    return pl.BlockSpec(shape, lambda i: (0,) * len(shape), pipeline_mode=pl.Buffered(1))


def attention_scratch(size, slot, width, heads, peers):
    dma = pltpu.SemaphoreType.DMA
    return [pltpu.VMEM((heads, slot, HEAD), BF16)] * 3 + [
        pltpu.VMEM((slot // size, heads * HEAD), BF16), pltpu.VMEM((heads, slot, slot), BF16)
    ] + [pltpu.VMEM((heads, slot, HEAD), F32)] * 2 + [
        pltpu.VMEM((width, heads * 3 * HEAD), BF16), pltpu.VMEM((heads * HEAD, width), BF16), dma((peers,)), dma((peers,)),
    ]


def opening_call(size, peers, length, x, weights, smalls, cos, sin, jobs):
    _, rows, width = x.shape
    slot, heads = rows * size, weights[0].shape[1] // (3 * HEAD)
    tile, pieces = 256, 4
    row_tiles, chips = slot // tile, peers // 2
    counts = [small.shape[0] for small in smalls]
    pack = (-(-len(counts) // 8) * 8, -(-max(counts) // 128) * 128)
    full = pl.BlockSpec(memory_space=pltpu.VMEM)
    dma = pltpu.SemaphoreType.DMA
    row_block = pl.BlockSpec((tile, width), lambda i: (jnp.minimum(i, row_tiles - 1), 0))
    ins, outs, scratch = job_lists(jobs)
    many = len(counts)
    n1, att, gp, xs, wa, wb, *rest = pl.pallas_call(
        partial(opening_kernel, size, peers, pieces, counts, jobs, row_tiles, heads, tile),
        grid=(row_tiles + heads + 1,),
        in_specs=[pl.BlockSpec(memory_space=pltpu.SMEM), HBM, HBM, HBM, whole(cos.shape), whole(sin.shape)]
        + [full] * many + [HBM] * len(ins),
        out_specs=[
            row_block, pl.BlockSpec((slot, HEAD), lambda i: (0, jnp.clip(i - row_tiles, 0, heads - 1))),
            whole((slot, heads * 3 * HEAD)), HBM, HBM, HBM,
        ] + [whole((1, peers * count)) for count in counts] + [HBM] * len(outs),
        out_shape=[
            jax.ShapeDtypeStruct((slot, width), BF16),
            jax.ShapeDtypeStruct((slot, heads * HEAD), BF16),
            jax.ShapeDtypeStruct((slot, heads * 3 * HEAD), BF16),
            jax.ShapeDtypeStruct((size, rows, width), x.dtype),
            *(jax.ShapeDtypeStruct((peers,) + weight.shape, x.dtype) for weight in weights),
        ] + [jax.ShapeDtypeStruct((1, peers * count), F32) for count in counts] + outs,
        scratch_shapes=attention_scratch(size, slot, width, heads, peers) + [
            pltpu.VMEM((2, tile, width), BF16), dma((2, tile // rows)),
        ] + gather_scratch(size, pieces) + [
            pltpu.VMEM(pack, F32), pltpu.VMEM((peers,) + pack, F32), dma((peers - 1,)), dma((peers - 1,)),
        ] + [dma((chips,)), dma((chips,)), dma((chips,)), dma((chips,)), dma] * 2 + scratch,
        compiler_params=pltpu.CompilerParams(
            dimension_semantics=("arbitrary",), vmem_limit_bytes=VMEM_BYTES, collective_id=0, has_side_effects=True,
        ),
        cost_estimate=pl.CostEstimate(flops=int(14e9), bytes_accessed=int(400e6), transcendentals=int(3e6)),
    )(length, x, *weights, cos, sin, *smalls, *ins)
    return n1, att, gp, rest[many:], xs.reshape(slot, width), wa.reshape(width, -1), wb, rest[:many]


def attention_call(number, size, length, x, wqkv, bqkv, wo, gain, shift, cos, sin, jobs):
    slot, width = x.shape
    heads = wqkv.shape[1] // (3 * HEAD)
    tile = 256
    row_tiles = slot // tile
    row_block = pl.BlockSpec((tile, width), lambda i: (jnp.minimum(i, row_tiles - 1), 0))
    clip = lambda first: lambda i: (0, jnp.clip(i - first, 0, heads - 1))
    ins, outs, scratch = job_lists(jobs)
    n1, att, gp, *given = pl.pallas_call(
        partial(attention_kernel, size, jobs, row_tiles, heads, tile),
        grid=(row_tiles + heads + 1,),
        in_specs=[
            pl.BlockSpec(memory_space=pltpu.SMEM), row_block, HBM, whole(bqkv.shape),
            HBM, whole(gain.shape), whole(shift.shape), whole(cos.shape), whole(sin.shape),
        ] + [HBM] * len(ins),
        out_specs=[
            row_block, pl.BlockSpec((slot, HEAD), clip(row_tiles)), whole((slot, heads * 3 * HEAD)),
        ] + [HBM] * len(outs),
        out_shape=[
            jax.ShapeDtypeStruct((slot, width), BF16),
            jax.ShapeDtypeStruct((slot, heads * HEAD), BF16),
            jax.ShapeDtypeStruct((slot, heads * 3 * HEAD), BF16),
        ] + outs,
        scratch_shapes=attention_scratch(size, slot, width, heads, wo.shape[0]) + scratch,
        compiler_params=pltpu.CompilerParams(
            dimension_semantics=("arbitrary",), vmem_limit_bytes=VMEM_BYTES, collective_id=number,
            has_side_effects=True,
        ),
        cost_estimate=pl.CostEstimate(flops=int(14e9), bytes_accessed=int(20e6), transcendentals=int(3e6)),
    )(length, x, wqkv, bqkv, wo, gain, shift, cos, sin, *ins)
    return n1, att, gp, given


def normal_pair(value):
    density = jnp.exp(-0.5 * value * value)
    t = 1.0 / (1.0 + (0.3275911 * math.sqrt(0.5)) * jnp.abs(value))
    series = ((((1.061405429 * t - 1.453152027) * t) + 1.421413741) * t - 0.284496736) * t + 0.254829592
    tail = (0.5 * t) * series * density
    return jnp.where(value >= 0, 1.0 - tail, tail), density * (1.0 / math.sqrt(2.0 * math.pi))


def feed_kernel(size, jobs, tile, chunk, steps, *refs):
    own, lines, _ = with_jobs(jobs, (13, 7, 7), refs)
    step = pl.program_id(0)
    w1_hbm, w2_hbm, wo_hbm, wqkv_hbm = own[5:9]
    xhat_s, w1_s, w2_s, wo_s, wqkv_s, w_sem, part_sem = own[20:]
    loads = [
        [pltpu.make_async_copy(w1_hbm, w1_s, w_sem.at[0])], side_by_side(w2_hbm, w2_s, part_sem.at[0]),
        side_by_side(wo_hbm, wo_s, part_sem.at[1]), [pltpu.make_async_copy(wqkv_hbm, wqkv_s, w_sem.at[1])],
    ]

    @pl.when(step == 0)
    def _():
        for copy in loads[0] + loads[1]:
            copy.start()
        greet([], [("tp", size)])
        for line in lines:
            line.start()
        for copy in loads[2] + loads[3]:
            copy.start()

    def ready(which):
        @pl.when(step == 0)
        def _():
            for copy in loads[which]:
                copy.wait()

    def hook(slot):
        for line in lines:
            spread(step, slot, 4, 4 * steps, line.steps())

    feed_body(hook, ready, tile, chunk, *own[:5], w1_s, w2_s, wo_s, wqkv_s, *own[9:20], xhat_s)

    @pl.when(step == steps - 1)
    def _():
        for line in lines:
            line.finish()


def feed_body(
    hook, ready, tile, chunk, len_ref, x_ref, c_ref, att_ref, gp_ref, w1_ref, w2_ref, wo_ref, wqkv_ref, b1_ref,
    gain1_ref, gain2_ref, shift2_ref, n2_ref, act_ref, gpre_ref, h_ref, u_ref, cot_s, sd_ref, xhat_s,
):
    step = pl.program_id(0)
    length = len_ref[0]
    hidden, model = w2_ref.shape

    @pl.when(step == 0)
    def _():
        sd_ref[...] = jnp.zeros_like(sd_ref)

    xhat, _ = row_stats(x_ref[...].astype(F32))
    xhat_s[...] = xhat
    n2_ref[...] = (xhat * gain2_ref[...] + shift2_ref[...]).astype(BF16)
    place = step * tile + lax.broadcasted_iota(jnp.int32, c_ref.shape, 0)
    cot_s[...] = jnp.where(place < length, c_ref[...], jnp.zeros_like(c_ref))
    ones = jnp.ones((8, tile), BF16)
    ready(0)
    for k in range(hidden // chunk):
        cols = slice(k * chunk, (k + 1) * chunk)
        pre = dot_nn(n2_ref[...], w1_ref[:, cols]) + b1_ref[:, cols]
        below, density = normal_pair(pre)
        act_ref[:, cols] = (pre * below).astype(BF16)
        if k == 0:
            ready(1)
        gact = dot_nt(cot_s[...], w2_ref[cols, :])
        gpre = (gact * (below + pre * density)).astype(BF16)
        gpre_ref[:, cols] = gpre
        sd_ref[5:6, cols] += dot_nn(ones, gpre)[0:1]
        if k == hidden // chunk // 2 - 1:
            hook(0)
    hook(1)
    sd_ref[6:7, 0:gp_ref.shape[1]] += dot_nn(ones, gp_ref[...])[0:1]
    ready(2)
    for k in range(model // chunk):
        cols = slice(k * chunk, (k + 1) * chunk)
        h_ref[:, cols] = (
            dot_nn(act_ref[...], w2_ref[:, cols]) + dot_nn(att_ref[...], wo_ref[:, cols])
        ).astype(BF16)
    ready(3)
    hook(2)
    for k in range(model // chunk):
        cols = slice(k * chunk, (k + 1) * chunk)
        g2 = dot_nt(gpre_ref[...], w1_ref[cols, :])
        g1 = dot_nt(gp_ref[...], wqkv_ref[cols, :])
        u_ref[:, cols] = (g1 * gain1_ref[:, cols] + g2 * gain2_ref[:, cols]).astype(BF16)
        hat = xhat_s[:, cols]
        sd_ref[0:1, cols] += jnp.sum(g1 * hat, axis=0, keepdims=True)
        sd_ref[1:2, cols] += jnp.sum(g1, axis=0, keepdims=True)
        sd_ref[2:3, cols] += jnp.sum(g2 * hat, axis=0, keepdims=True)
        sd_ref[3:4, cols] += jnp.sum(g2, axis=0, keepdims=True)
        sd_ref[4:5, cols] += dot_nn(ones, cot_s[:, cols])[0:1]
    hook(3)


def feed_call(number, size, length, x, c, att, gp, w1, w2, wo, wqkv, b1, gain1, gain2, shift2, jobs):
    slot, width = x.shape
    ins, outs, scratch = job_lists(jobs)
    hidden = w1.shape[1]
    tile, chunk = 256, 512
    at = lambda i: (i, 0)
    keep = lambda i: (0, 0)
    row_block = pl.BlockSpec((tile, width), at)
    hid_block = pl.BlockSpec((tile, hidden), at)
    out = pl.pallas_call(
        partial(feed_kernel, size, jobs, tile, chunk, slot // tile),
        grid=(slot // tile,),
        in_specs=[
            pl.BlockSpec(memory_space=pltpu.SMEM), row_block, row_block, pl.BlockSpec((tile, att.shape[1]), at),
            pl.BlockSpec((tile, gp.shape[1]), at), HBM, HBM, HBM, HBM, whole(b1.shape), whole(gain1.shape), whole(gain2.shape), whole(shift2.shape),
        ] + [HBM] * len(ins),
        out_specs=[
            row_block, hid_block, hid_block, row_block, row_block, row_block, pl.BlockSpec((8, width), keep),
        ] + [HBM] * len(outs),
        out_shape=[
            jax.ShapeDtypeStruct((slot, width), BF16),
            jax.ShapeDtypeStruct((slot, hidden), BF16),
            jax.ShapeDtypeStruct((slot, hidden), BF16),
            jax.ShapeDtypeStruct((slot, width), BF16),
            jax.ShapeDtypeStruct((slot, width), BF16),
            jax.ShapeDtypeStruct((slot, width), BF16),
            jax.ShapeDtypeStruct((8, width), F32),
        ] + outs,
        scratch_shapes=[
            pltpu.VMEM((tile, width), F32), pltpu.VMEM(w1.shape, BF16), pltpu.VMEM((hidden, width), BF16),
            pltpu.VMEM((att.shape[1], width), BF16), pltpu.VMEM(wqkv.shape, BF16), pltpu.SemaphoreType.DMA((2,)),
            pltpu.SemaphoreType.DMA((2, w2.shape[0])),
        ] + scratch,
        compiler_params=pltpu.CompilerParams(
            dimension_semantics=("arbitrary",), vmem_limit_bytes=VMEM_BYTES, collective_id=number,
            has_side_effects=True,
        ),
        cost_estimate=pl.CostEstimate(flops=int(45e9), bytes_accessed=int(50e6), transcendentals=int(4e6)),
    )(length, x, c, att, gp, w1, w2, wo, wqkv, b1, gain1, gain2, shift2, *ins)
    return (*out[:7], out[7:])

LAG = 1
RING = 8


def grads_kernel(size, peers, micros, jobs, *refs):
    before = micros - 1
    own_refs, sums, _ = with_jobs(jobs, (8 * micros + 5 + 4 * before, 4 + 2 * before, 29), refs)
    take = iter(own_refs)
    lefts = [[next(take) for _ in range(micros)] for _ in range(3)]
    rights = [[next(take) for _ in range(micros)] for _ in range(4)]
    vecs = [next(take) for _ in range(micros)]
    len_ref, x_ref, c_ref, bo_ref, b2_ref = [next(take) for _ in range(5)]
    earlier = [[next(take) for _ in range(4)] for _ in range(before)]
    out_ref, turned_ref, vec_ref, vec_tp_ref = [next(take) for _ in range(4)]
    ended = [[next(take) for _ in range(2)] for _ in range(before)]
    (a_buf, b_buf, p_s, ex_send, ex_recv, out_send, recv, acc, acc_t, vec_s, vec_all, vec_line,
     a_sem, b_sem, ex_ssem, ex_rsem, out_ssem, out_rsem, w_sem, v_ssem, v_rsem, l_ssem, l_rsem,
     row_s, last_s, end_s, row_sem, last_sem, end_sem) = take
    here, line = lax.axis_index("fsdp"), lax.axis_index("tp")
    chip, core = here // 2, lax.rem(here, 2)
    chips = peers // 2
    own, wide = acc.shape[1:]
    slot = a_buf.shape[1] // micros
    chunks = acc.shape[0]
    total = chunks * chips
    firsts = [0, rights[0][0].shape[1] // wide]
    firsts.append(firsts[1] + rights[1][0].shape[1] // wide)
    firsts.append(firsts[2] + rights[2][0].shape[1] // wide)
    firsts.append(chunks)
    left_of = [0, 1, 1, 2]

    def split(unit):
        return unit // chips, lax.rem(unit, chips)

    def target(s):
        return lax.rem(chip + 1 + s, chips)

    def a_copy(group, m, unit):
        cols = pl.ds(pl.multiple_of(target(split(unit)[1]) * (2 * own), 2 * own), 2 * own)
        at = lax.rem(unit, 2)
        return pltpu.make_async_copy(
            lefts[left_of[group]][m].at[:, cols], a_buf.at[at, pl.ds(m * slot, slot)], a_sem.at[at, m]
        )

    def b_copy(group, m, chunk):
        cols = pl.ds(pl.multiple_of((chunk - firsts[group]) * wide, wide), wide)
        at = lax.rem(chunk, 2)
        return pltpu.make_async_copy(
            rights[group][m].at[:, cols], b_buf.at[at, pl.ds(m * slot, slot)], b_sem.at[at, m]
        )

    def in_group(chunk, do):
        for group in range(4):
            @pl.when((chunk >= firsts[group]) & (chunk < firsts[group + 1]))
            def _():
                for m in range(micros):
                    do(group, m)

    def exchange(unit):
        at = lax.rem(unit, RING)
        return pltpu.make_async_remote_copy(
            ex_send.at[at], ex_recv.at[at], ex_ssem.at[at], ex_rsem.at[at],
            device_id={"fsdp": 2 * chip + 1 - core}, device_id_type=MESH,
        )

    def passing(place, s):
        return pltpu.make_async_remote_copy(
            out_send.at[place], recv.at[place], out_ssem.at[place], out_rsem.at[place],
            device_id={"fsdp": 2 * target(s) + core}, device_id_type=MESH,
        )

    def process(unit):
        chunk, s = split(unit)
        exchange(unit).wait_recv()
        both = p_s[lax.rem(unit, 4), pl.ds(core * own, own), :] + ex_recv[lax.rem(unit, RING)].astype(F32)

        @pl.when(s < chips - 1)
        def _():
            place = chunk * (chips - 1) + s
            out_send[place] = both.astype(BF16)
            passing(place, s).start()

        @pl.when(s == chips - 1)
        def _():
            acc[chunk] = both

    def vec_copy(k, there):
        return pltpu.make_async_remote_copy(
            vec_s, vec_all.at[there], v_ssem.at[k - 1], v_rsem.at[k - 1],
            device_id={"fsdp": lax.rem(here + k, peers)}, device_id_type=MESH,
        )

    def line_copy(k, there):
        return pltpu.make_async_remote_copy(
            vec_ref, vec_line.at[there], l_ssem.at[k - 1], l_rsem.at[k - 1],
            device_id={"tp": lax.rem(line + k, size)}, device_id_type=MESH,
        )

    in_group(0, lambda group, m: b_copy(group, m, 0).start())
    in_group(0, lambda group, m: a_copy(group, m, 0).start())
    greet([("fsdp", peers), ("tp", size)], [])
    vec = vecs[0][...]
    for more in vecs[1:]:
        vec = vec + more[...]
    vec_s[...] = vec
    vec_all[here] = vec
    for k in range(1, peers):
        vec_copy(k, here).start()
    for one in sums:
        one.start()
    hooks = [act for acts in zip(*(one.steps() for one in sums)) for act in acts]
    span = total + 3 * chunks
    due = [(i // len(sums) + 1) * span * len(sums) // (len(hooks) + len(sums) * 2) + 2 for i in range(len(hooks))]

    def body(unit, carry):
        chunk, s = split(unit)
        after = unit + 1

        @pl.when(after < total)
        def _():
            in_group(after // chips, lambda group, m: a_copy(group, m, after).start())

        @pl.when((s == 0) & (chunk + 1 < chunks))
        def _():
            in_group(chunk + 1, lambda group, m: b_copy(group, m, chunk + 1).start())

        for m in range(micros):
            a_copy(0, m, unit).wait()

        @pl.when(s == 0)
        def _():
            for m in range(micros):
                pltpu.make_async_copy(
                    rights[0][m].at[:, pl.ds(0, wide)], b_buf.at[lax.rem(chunk, 2), pl.ds(m * slot, slot)],
                    b_sem.at[lax.rem(chunk, 2), m],
                ).wait()

        p_s[lax.rem(unit, 4)] = dot_tn(a_buf[lax.rem(unit, 2)], b_buf[lax.rem(chunk, 2)])

        @pl.when(unit >= RING)
        def _():
            exchange(unit).wait_send()

        ex_send[lax.rem(unit, RING)] = p_s[lax.rem(unit, 4), pl.ds((1 - core) * own, own), :].astype(BF16)
        exchange(unit).start()

        @pl.when(unit >= LAG)
        def _():
            process(unit - LAG)

        for i, act in enumerate(hooks):
            if due[i] < total:
                @pl.when(unit == due[i])
                def _():
                    act()

        return carry

    lax.fori_loop(0, total, body, 0)
    lax.fori_loop(total - LAG, total, lambda unit, carry: (process(unit), carry)[1], 0)

    for k in range(1, peers):
        vec_copy(k, lax.rem(here + peers - k, peers)).wait_recv()
        vec_copy(k, here).wait_send()
    vec = vec_all[0]
    for k in range(1, peers):
        vec = vec + vec_all[k]
    vec_ref[...] = vec
    vec_line[line] = vec
    for k in range(1, size):
        line_copy(k, line).start()

    step = end_s.shape[1]

    def end_step(m, k):
        at = pl.ds(k * step, step)
        h, u, h_last, u_last = earlier[m]
        loads = [
            pltpu.make_async_copy(source, row_s.at[i], row_sem.at[i])
            for i, source in enumerate((x_ref.at[m, at], c_ref.at[m, at], h.at[line, at], u.at[line, at]))
        ] + [
            pltpu.make_async_copy(source.at[:, at], last_s.at[i], last_sem.at[i])
            for i, source in enumerate((h_last, u_last))
        ]
        for copy in loads:
            copy.start()
        for copy in loads:
            copy.wait()
        local = row_s[0].astype(F32)
        place = line * x_ref.shape[1] + k * step + lax.broadcasted_iota(jnp.int32, local.shape, 0)
        y, dx = end_rows(
            local, line_total(line, size, row_s[2], last_s[0, 0], last_s[0, 1]),
            line_total(line, size, row_s[3], last_s[1, 0], last_s[1, 1]), row_s[1].astype(F32),
            place < len_ref[m, 0], bo_ref[...] + b2_ref[...],
        )
        end_s[0], end_s[1] = y, dx
        stores = [pltpu.make_async_copy(end_s.at[i], ended[m][i].at[at], end_sem.at[i]) for i in range(2)]
        for copy in stores:
            copy.start()
        for copy in stores:
            copy.wait()

    for m in range(before):
        lax.fori_loop(0, x_ref.shape[1] // step, lambda k, carry: (end_step(m, k), carry)[1], 0)

    def finish(chunk, carry):
        for i, act in enumerate(hooks):
            if due[i] >= total:
                @pl.when(chunk == min((due[i] - total) // 3, chunks - 1))
                def _():
                    act()

        value = acc[chunk]
        for s in range(chips - 1):
            place = chunk * (chips - 1) + s
            passing(place, s).wait_recv()
            value = value + recv[place].astype(F32)
        turned = (chunk >= firsts[1]) & (chunk < firsts[3])

        @pl.when(turned)
        def _():
            acc_t[chunk - firsts[1]] = value.T
            turn_out(chunk).start()

        @pl.when(jnp.logical_not(turned))
        def _():
            acc[chunk] = value
            plain_out(chunk).start()

        return carry

    def turn_out(chunk):
        at = chunk - firsts[1]
        return pltpu.make_async_copy(acc_t.at[at], turned_ref.at[at], w_sem.at[chunk])

    def plain_out(chunk):
        return pltpu.make_async_copy(acc.at[chunk], out_ref.at[chunk], w_sem.at[chunk])

    lax.fori_loop(0, chunks, finish, 0)
    for k in range(1, size):
        line_copy(k, lax.rem(line + size - k, size)).wait_recv()
        line_copy(k, line).wait_send()
    vec = vec_line[0]
    for k in range(1, size):
        vec = vec + vec_line[k]
    vec_tp_ref[...] = vec

    def close(chunk, carry):
        for s in range(chips - 1):
            passing(chunk * (chips - 1) + s, s).wait_send()
        plain_out(chunk).wait()
        return carry

    lax.fori_loop(0, chunks, close, 0)
    for one in sums:
        one.finish()
    lax.fori_loop(total - RING, total, lambda unit, carry: (exchange(unit).wait_send(), carry)[1], 0)


def grads_call(number, size, peers, lefts, rights, vecs, ends, earlier, jobs):
    micros = len(vecs)
    rows = ends[1].shape[1]
    step = min(64, rows)
    before = [x for group in earlier for x in group]
    slot, model = lefts[0][0].shape
    ins, outs, scratch = job_lists(jobs)
    own, wide = model // peers, rights[2][0].shape[1]
    chunks = sum(group[0].shape[1] for group in rights) // wide
    turned = sum(group[0].shape[1] for group in rights[1:3]) // wide
    chips = peers // 2
    full = pl.BlockSpec(memory_space=pltpu.VMEM)
    vec = jax.ShapeDtypeStruct(vecs[0].shape, F32)
    places = chunks * (chips - 1)
    dma = pltpu.SemaphoreType.DMA
    flat = [x for group in (*lefts, *rights) for x in group]
    return pl.pallas_call(
        partial(grads_kernel, size, peers, micros, jobs),
        in_specs=[HBM] * len(flat) + [full] * micros + [
            pl.BlockSpec(memory_space=pltpu.SMEM), HBM, HBM, full, full
        ] + [HBM] * len(before) + [HBM] * len(ins),
        out_specs=[HBM, HBM, full, full] + [HBM] * (2 * len(earlier)) + [HBM] * len(outs),
        out_shape=[
            jax.ShapeDtypeStruct((chunks, own, wide), F32), jax.ShapeDtypeStruct((turned, wide, own), F32), vec, vec
        ]
        + [jax.ShapeDtypeStruct((rows, model), BF16)] * (2 * len(earlier)) + outs,
        scratch_shapes=[
            pltpu.VMEM((2, micros * slot, 2 * own), BF16), pltpu.VMEM((2, micros * slot, wide), BF16),
            pltpu.VMEM((4, 2 * own, wide), F32), pltpu.VMEM((RING, own, wide), BF16),
            pltpu.VMEM((RING, own, wide), BF16), pltpu.VMEM((places, own, wide), BF16),
            pltpu.VMEM((places, own, wide), BF16), pltpu.VMEM((chunks, own, wide), F32),
            pltpu.VMEM((turned, wide, own), F32),
            pltpu.VMEM(vec.shape, F32), pltpu.VMEM((peers,) + vec.shape, F32), pltpu.VMEM((size,) + vec.shape, F32),
            dma((2, micros)), dma((2, micros)), dma((RING,)), dma((RING,)), dma((places,)), dma((places,)),
            dma((chunks,)), dma((peers - 1,)), dma((peers - 1,)), dma((size - 1,)), dma((size - 1,)),
            pltpu.VMEM((4, step, model), BF16), pltpu.VMEM((2, 2, step, model), BF16),
            pltpu.VMEM((2, step, model), BF16), dma((4,)), dma((2,)), dma((2,)),
        ] + scratch,
        compiler_params=pltpu.CompilerParams(
            collective_id=number, has_side_effects=True, vmem_limit_bytes=VMEM_BYTES
        ),
        cost_estimate=pl.CostEstimate(flops=int(52e9), bytes_accessed=int(200e6), transcendentals=0),
    )(*flat, *vecs, *ends, *before, *ins)


def end_rows(local, h, u, cot, live, shift):
    xhat, rstd = row_stats(local)
    back = rstd * (u - jnp.mean(u, axis=-1, keepdims=True) - xhat * jnp.mean(u * xhat, axis=-1, keepdims=True))
    return (
        jnp.where(live, local + h + shift, 0.0).astype(BF16), (jnp.where(live, cot, 0.0) + back).astype(BF16),
    )


def line_total(here, size, own, left, right):
    value = own.astype(F32) + jnp.where(here > 0, left.astype(F32), 0.0)
    return value + jnp.where(here < size - 1, right.astype(F32), 0.0)


def close_kernel(
    size, hidden, peers, micros, len_ref, x_ref, c_ref, bo_ref, b2_ref, vec_ref, vec_tp_ref, g_ref, turned_ref, *refs,
):
    before = micros - 1
    h_ref, u_ref, h_last, u_last = refs[:4]
    ended, refs = refs[4:4 + 2 * before], refs[4 + 2 * before:]
    y_ref, dx_ref, up_ref, down_ref, out_ref, qkv_ref = refs[:6]
    rows_out = refs[6:14]
    row_s, last_s, g_s, t_s, row_sem, g_sem, done_sem = refs[14:]
    here = lax.axis_index("tp")
    chunks, own, wide = g_ref.shape
    dma = pltpu.make_async_copy
    plain = [*range(hidden), *range(2 * hidden + 1, chunks)]
    arrive = [dma(g_ref.at[b], g_s.at[i], g_sem.at[b]) for i, b in enumerate(plain)]
    arrive += [dma(turned_ref.at[b], t_s.at[b], g_sem.at[hidden + b]) for b in range(hidden + 1)]
    loads = [
        dma(source, row_s.at[i], row_sem.at[i])
        for i, source in enumerate((x_ref.at[before], c_ref.at[before], h_ref.at[here], u_ref.at[here]))
    ] + [dma(source, last_s.at[i], row_sem.at[4 + i]) for i, source in enumerate((h_last, u_last))]
    copies = [
        dma(ended[2 * m + k], (y_ref, dx_ref)[k].at[m], done_sem.at[2 * m + k]) for m in range(before) for k in range(2)
    ]
    for copy in arrive + loads + copies:
        copy.start()
    sources = [(vec_tp_ref, k) for k in range(4)] + [(vec_ref, k) for k in (4, 4, 5, 6)]
    for peer in range(peers):
        @pl.when(lax.axis_index("fsdp") == peer)
        def _():
            for goal, (source, row) in zip(rows_out, sources):
                count = goal.shape[0]
                goal[...] = source[row:row + 1, peer * count:(peer + 1) * count].reshape(count)

    rows = row_s.shape[1]
    step = min(64, rows)

    def end_step(k, carry):
        at = pl.ds(k * step, step)
        local = row_s[0, at].astype(F32)
        place = here * rows + k * step + lax.broadcasted_iota(jnp.int32, local.shape, 0)
        y_ref[before, at], dx_ref[before, at] = end_rows(
            local, line_total(here, size, row_s[2, at], last_s[0, 0, at], last_s[0, 1, at]),
            line_total(here, size, row_s[3, at], last_s[1, 0, at], last_s[1, 1, at]), row_s[1, at].astype(F32),
            place < len_ref[before, 0], bo_ref[...] + b2_ref[...],
        )
        return carry

    ends = []
    for i, b in enumerate(plain):
        goal, at = (up_ref, b) if b < hidden else (qkv_ref, b - 2 * hidden - 1)
        ends.append(dma(g_s.at[i], goal.at[:, pl.ds(at * wide, wide)], g_sem.at[b]))
    for b in range(hidden + 1):
        goal = down_ref.at[pl.ds(b * wide, wide)] if b < hidden else out_ref
        ends.append(dma(t_s.at[b], goal, g_sem.at[hidden + b]))
    for came, leaves in zip(arrive, ends):
        came.wait()
        leaves.start()
    for copy in loads:
        copy.wait()
    lax.fori_loop(0, rows // step, end_step, 0)
    for copy in copies + ends:
        copy.wait()


def close_call(size, peers, lengths, x, c, bo, b2, vec, vec_tp, grads, turned, sides, lasts, ended, counts):
    micros, rows, width = x.shape
    chunks, own, wide = grads.shape
    hidden = (chunks - 4) // 2
    full = pl.BlockSpec(memory_space=pltpu.VMEM)
    dma = pltpu.SemaphoreType.DMA
    return pl.pallas_call(
        partial(close_kernel, size, hidden, peers, micros),
        in_specs=[pl.BlockSpec(memory_space=pltpu.SMEM), HBM, HBM, full, full, full, full, HBM, HBM]
        + [HBM] * (4 + len(ended)),
        out_specs=[full, full, HBM, HBM, HBM, HBM] + [full] * 8,
        out_shape=[
            jax.ShapeDtypeStruct(x.shape, BF16), jax.ShapeDtypeStruct(x.shape, BF16),
            jax.ShapeDtypeStruct((own, hidden * wide), F32), jax.ShapeDtypeStruct((hidden * wide, own), F32),
            jax.ShapeDtypeStruct((wide, own), F32), jax.ShapeDtypeStruct((own, 3 * wide), F32),
        ] + [jax.ShapeDtypeStruct((count,), F32) for count in counts],
        scratch_shapes=[
            pltpu.VMEM((4, rows, width), BF16), pltpu.VMEM((2, 2, rows, width), BF16),
            pltpu.VMEM((hidden + 3, own, wide), F32), pltpu.VMEM((hidden + 1, wide, own), F32),
            dma((6,)), dma((chunks,)), dma((max(len(ended), 1),)),
        ],
        compiler_params=pltpu.CompilerParams(vmem_limit_bytes=VMEM_BYTES),
        cost_estimate=pl.CostEstimate(flops=0, bytes_accessed=int(36e6), transcendentals=0),
    )(lengths, x, c, bo, b2, vec, vec_tp, grads, turned, *sides, *lasts, *ended)


def shards(
    hidden_in, out_grad, lengths, qkv_weight, qkv_bias, out_weight, out_bias, fc1_weight, fc1_bias,
    fc2_weight, fc2_bias, ln1_gain, ln1_bias, ln2_gain, ln2_bias,
):
    tp_size = lax.axis_size("tp")
    fsdp_index = lax.axis_index("fsdp")
    micro_count, shard_rows, model = hidden_in.shape
    slot = shard_rows * tp_size
    own = out_bias.shape[0]
    cos, sin = rotary_full(slot)
    gather = lambda value, axis: lax.all_gather(value, axis, axis=0, tiled=True)

    small = (qkv_bias, fc1_bias, out_bias, fc2_bias, ln1_gain, ln1_bias, ln2_gain, ln2_bias)
    peers = lax.axis_size("fsdp")
    w1 = gather(fc1_weight, "fsdp")
    w2 = lax.all_gather(fc2_weight, "fsdp", axis=0, tiled=False)

    parts, sides, lasts = [], [], []
    for m in range(micro_count):
        length = lengths[m]
        jobs = [landing_job(tp_size, 2, out_grad, m)]
        if m:
            jobs.append(reduce_job(tp_size, 2, sides[m - 1][0]))
        if m == 0:
            n1, att, gp, (c, *last), x, wqkv, wo, vectors = opening_call(
                tp_size, peers, length, hidden_in, (qkv_weight, out_weight), small, cos, sin, jobs
            )
            bqkv, b1, bo, b2, gain1, shift1, gain2, shift2 = vectors
        else:
            n1, att, gp, (c, *last) = attention_call(
                1 + 2 * m, tp_size, length, x, wqkv, bqkv, wo, gain1, shift1, cos, sin, jobs
            )
        jobs = [reduce_job(tp_size, 2, sides[m - 1][1])] if m else []
        if m + 1 < micro_count:
            jobs.append(gather_job(tp_size, 2, hidden_in, m + 1))
        n2, act, gpre, h, u, cot, sums, given = feed_call(
            2 + 2 * m, tp_size, length, x, c.reshape(slot, model), att, gp, w1, w2, wo, wqkv, b1, gain1, gain2,
            shift2, jobs,
        )
        if m:
            lasts.append((*last, given[0]))
        parts.append((n2, cot, n1, gpre, act, att, gp, sums))
        sides.append((h, u))
        if m + 1 < micro_count:
            x = given[-1].reshape(slot, model)

    by_kind = [list(kind) for kind in zip(*parts)]
    sides = [[side.reshape(tp_size, shard_rows, model) for side in pair] for pair in sides]
    grads, turned, vec, vec_tp, *rest = grads_call(
        1 + 2 * micro_count, tp_size, peers, by_kind[0:3], by_kind[3:7], by_kind[7],
        (lengths, hidden_in, out_grad, bo, b2), [(*side, *last) for side, last in zip(sides, lasts)],
        [reduce_job(tp_size, 2, side.reshape(slot, model)) for side in sides[-1]],
    )
    ended, last = rest[:-2], rest[-2:]
    y, dx, grad_up, grad_down, grad_out, grad_qkv, *rows = close_call(
        tp_size, peers, lengths, hidden_in, out_grad, bo, b2, vec, vec_tp, grads, turned, sides[-1], last, ended,
        [own] * 6 + [fc1_bias.shape[0], qkv_bias.shape[0]],
    )
    ln, grad_bias, grad_bias_two, grad_b1, grad_bq = rows[:4], *rows[4:]
    return (
        y, dx, grad_qkv, grad_bq, grad_out, grad_bias, grad_up, grad_b1,
        grad_down, grad_bias_two, ln[0], ln[1], ln[2], ln[3],
    )


def solution(mesh):
    rows = P(None, ("fsdp", "tp"), None)
    both, column, row, one = P(("tp", "fsdp")), P("fsdp", "tp"), P("tp", "fsdp"), P("fsdp")
    return jax.shard_map(
        shards,
        mesh=mesh,
        in_specs=(rows, rows, P(None, "fsdp"), column, both, row, one, column, both, row, one, one, one, one, one),
        out_specs=(rows, rows, column, both, row, one, column, both, row, one, one, one, one, one),
        check_vma=False,
    )
```
